32 devices in a mesh: grp: 2 (over x), row: 8 (over z, y), col: 2 (over core).
Axes of the slice: x: 2, y: 2, z: 4, core: 2. Of those that a mesh axis runs over, the one named last changes fastest.
Arguments:
- embeddings: bfloat16 [16384, 128], P(('grp', 'row')), parts along dimension 0, may hold values from -6 to 6
- profiles: float32 [16384, 128], P(('grp', 'row')), parts along dimension 0, may hold values from -16 to 16
- seed_mask: int32 [16384], P(('grp', 'row')), parts along dimension 0, may hold values 0 or 1
- tile_cols: int32 [32, 13], P(('grp', 'row')), parts along dimension 0, may hold values from 0 to 15, as said below
- tile_count: int32 [32], P(('grp', 'row')), parts along dimension 0, may hold values from 1 to 13, as said below
Outputs:
- spread: float32 [16384, 128], P(('grp', 'row')), parts along dimension 0
The draws below stay inside these ranges and needn't reach their ends.
There are 2 independent parts, one for each index of `grp`. The reference program is written for one: setup_inputs(seed, part) draws one part's arguments, and reference() takes and returns one part's arrays. A program takes and returns all parts, laid end to end along the dimension named above; each array names one. Nothing has to cross between parts.
Inputs may be any that keep to these rules, and one draw needn't show every extreme that they name: `tile_cols`: row block b lists itself in slot 0; slots 1 to tile_count[b] - 1 hold distinct other blocks c with |c - b| <= 6; later slots repeat b and are no tiles. `tile_count`: some row block lists 13 tiles and some lists one.
All inputs are finite; a program needn't handle non-finite values. No bound on the sum of `seed_mask` on one device may be relied on, other than what follows from the above.
Results may differ from the reference program's by a relative error of at most 0.00083.
Values may be sent and summed in bfloat16 or wider, within the bound.
No kernel may reach another device: no remote copies, remote signals or barrier semaphores. Data moves between devices by JAX's collectives and lax.ppermute only.
A program may use at most 64 MiB of HBM per device.

```python
import jax
import jax.numpy as jnp
from jax import lax

EMB = 128
PROF = 128
BAND = 6
ITERS = 2
BLOCKS = 16
MOLS = 8192


def tile_table(key):
    shared = jax.random.fold_in(key, 7)
    first_key, second_key = jax.random.split(shared)
    block_ids = jnp.arange(BLOCKS, dtype=jnp.int32)
    offsets = jnp.concatenate([jnp.arange(-BAND, 0, dtype=jnp.int32), jnp.arange(1, BAND + 1, dtype=jnp.int32)])
    target_labels = block_ids[:, None] + offsets[None, :]
    inside = jnp.logical_and(target_labels >= 0, target_labels < BLOCKS)
    scores = jax.random.randint(first_key, (BLOCKS, 2 * BAND), 0, 1 << 20) * (2 * BAND) + jnp.arange(2 * BAND, dtype=jnp.int32)[None, :]
    scores = jnp.where(inside, scores, scores + (1 << 26))
    rank_order = jnp.argsort(scores, axis=1, stable=True)
    chosen = jnp.take_along_axis(target_labels, rank_order, axis=1)
    ready_tiles = jnp.sum(inside.astype(jnp.int32), axis=1)
    surplus_tiles = jnp.minimum(jax.random.randint(second_key, (BLOCKS,), 0, 2 * BAND + 1), ready_tiles)
    surplus_tiles = jnp.where(block_ids == BLOCKS // 2, ready_tiles, surplus_tiles)
    surplus_tiles = jnp.where(block_ids == 0, ready_tiles, surplus_tiles)
    surplus_tiles = jnp.where(block_ids == BLOCKS // 4, 0, surplus_tiles)
    counts = surplus_tiles + 1
    listing = jnp.concatenate([block_ids[:, None], chosen], axis=1)
    slot_ids = jnp.arange(2 * BAND + 1, dtype=jnp.int32)
    listing = jnp.where(slot_ids[None, :] < counts[:, None], listing, block_ids[:, None])
    return (listing.astype(jnp.int32), counts.astype(jnp.int32))


def draw_tile_cols(key, part):
    return tile_table(key)[0]


def draw_tile_count(key, part):
    return tile_table(key)[1]


def with_ends(entries, stream_key, smallest, top_value):
    shape = entries.shape
    place = [jax.random.randint(jax.random.fold_in(stream_key, axis), (), 0, shape[axis]) for axis in range(len(shape))]
    entries = entries.at[tuple(place)].set(smallest)
    longest = shape.index(max(shape))
    place[longest] = (place[longest] + 1) % shape[longest]
    return entries.at[tuple(place)].set(top_value)


def block_levels(rng, shape, shards, low, high):
    def one(dim, blocks):
        steps = jax.random.uniform(jax.random.fold_in(jax.random.fold_in(rng, 6), dim), (blocks,), jnp.float32, low / len(shards), high / len(shards))
        return jnp.repeat(jnp.exp(steps), shape[dim] // blocks).reshape((-1,) + (1,) * (len(shape) - dim - 1))

    factor_of = one(*shards[0])
    for cut in shards[1:]:
        factor_of = factor_of * one(*cut)
    return factor_of


def bell_draw(own_key, extent, width, reach, shards=(), held_as=jnp.bfloat16):
    values = width * jax.random.normal(own_key, extent, jnp.float32)
    if shards:
        values = values * block_levels(own_key, extent, shards, -0.22, 0.18)
    return jnp.clip(values, -reach, reach).astype(held_as)


def setup_inputs(seed: int = 0, part: int = 0) -> dict:
    arg_keys = jax.random.split(jax.random.key(seed), 6)
    part_splits = jax.random.split(jax.random.fold_in(arg_keys[5], part), 6)
    embeddings = bell_draw(part_splits[0], (MOLS, EMB), 1.0, 6.0, ((0, 8),))
    profiles = bell_draw(part_splits[1], (MOLS, PROF), 3.0, 16.0, ((0, 8),), jnp.float32)
    seed_mask = with_ends((jax.random.randint(part_splits[2], (MOLS,), 0, 2) < 1).astype(jnp.int32), jax.random.fold_in(part_splits[2], 1), 0, 1)
    tile_cols = draw_tile_cols(jax.random.fold_in(jax.random.fold_in(arg_keys[5], part), 71), part)
    tile_count = draw_tile_count(jax.random.fold_in(jax.random.fold_in(arg_keys[5], part), 71), part)
    return {"embeddings": embeddings, "profiles": profiles, "seed_mask": seed_mask, "tile_cols": tile_cols, "tile_count": tile_count}


KERNEL_SCALE = 12.5
ALPHA = 0.8
EPS = 1e-06

def reference(embeddings, profiles, seed_mask, tile_cols, tile_count):
    blocks = tile_cols.shape[0]
    slot_total = tile_cols.shape[1]
    block_rows = embeddings.shape[0] // blocks
    emb_width = embeddings.shape[1]
    prof_width = profiles.shape[1]
    embedding_blocks = embeddings.reshape(blocks, block_rows, emb_width)
    values = embeddings.astype(jnp.float32)
    inv_norm = lax.rsqrt(lax.optimization_barrier(jnp.mean(values * values, axis=1)) + EPS).reshape(blocks, block_rows)
    seed_rows = (seed_mask.astype(jnp.float32)[:, None] * profiles).reshape(blocks, block_rows, prof_width)
    local_ids = jnp.arange(block_rows, dtype=jnp.int32)
    slot_ids = jnp.arange(slot_total, dtype=jnp.int32)
    block_ids = jnp.arange(blocks, dtype=jnp.int32)

    def kernel_matrix(row_block, col_block):
        row_tile = embedding_blocks[row_block]
        col_tile = embedding_blocks[col_block]
        cosine_similarity = jnp.dot(row_tile, col_tile.T, preferred_element_type=jnp.float32) * inv_norm[row_block][:, None] * inv_norm[col_block][None, :] / emb_width
        edge_weight = jnp.exp((cosine_similarity - 1.0) * (2.0 * KERNEL_SCALE))
        row_ids = row_block * block_rows + local_ids
        col_ids = col_block * block_rows + local_ids
        return jnp.where(row_ids[:, None] == col_ids[None, :], 0.0, edge_weight)

    def degree_block(col_sums, row_block):
        live_count = tile_count[row_block]

        def add_slot(sums_carry, slot_index):
            col_block = tile_cols[row_block, slot_index]

            def add_tile(inner):
                row_sum, col_part = inner
                edge_weight = kernel_matrix(row_block, col_block)
                return (row_sum + lax.optimization_barrier(jnp.sum(edge_weight, axis=1)), col_part.at[col_block].add(lax.optimization_barrier(jnp.sum(edge_weight, axis=0))))
            return (lax.cond(slot_index < live_count, add_tile, lambda unchanged: unchanged, sums_carry), None)
        (row_sum, col_sums), _ = lax.scan(add_slot, (jnp.zeros((block_rows,), jnp.float32), col_sums), slot_ids)
        return (col_sums, row_sum)
    col_degree, row_degree = lax.scan(degree_block, jnp.zeros((blocks, block_rows), jnp.float32), block_ids)
    col_scale = lax.rsqrt(col_degree)
    row_scale = lax.rsqrt(row_degree)

    def products(scaled):

        def product_block(row_block):
            live_count = tile_count[row_block]

            def add_slot(row_total, slot_index):
                col_block = tile_cols[row_block, slot_index]

                def add_tile(inner):
                    edge_weight = kernel_matrix(row_block, col_block).astype(jnp.bfloat16)
                    return inner + jnp.dot(edge_weight, scaled[col_block], preferred_element_type=jnp.float32)
                return (lax.cond(slot_index < live_count, add_tile, lambda unchanged: unchanged, row_total), None)
            row_total, _ = lax.scan(add_slot, jnp.zeros((block_rows, prof_width), jnp.float32), slot_ids)
            return row_total
        return lax.map(product_block, block_ids)
    spread_state = seed_rows
    for iteration in range(ITERS):
        scaled = (spread_state * col_scale[:, :, None]).astype(jnp.bfloat16)
        product = products(scaled)
        spread_state = ALPHA * product * row_scale[:, :, None] + (1.0 - ALPHA) * seed_rows
    return spread_state.reshape(blocks * block_rows, prof_width)
```

```python
import jax
import jax.numpy as jnp
from jax import lax
from jax.experimental import pallas as pl
from jax.experimental.pallas import tpu as pltpu
from jax.sharding import PartitionSpec as P

BAND = 6
ITERS = 2

KERNEL_SCALE = 12.5
ALPHA = 0.8
EPS = 1e-06
LOG2E = 1.4426950408889634
LANES = 128
F32 = jnp.float32
BF16 = jnp.bfloat16

VMEM = pl.BlockSpec(memory_space=pltpu.VMEM)
SMEM = pl.BlockSpec(memory_space=pltpu.SMEM)


def peer_pairs(rows, cols, distance):
    pairs = []
    for low in range(rows - distance):
        core = (low // distance) % cols
        a, b = low * cols + core, (low + distance) * cols + core
        pairs += [(a, b), (b, a)]
    return pairs


def peer_sign(row_dev, col_dev, distance):
    return jnp.where(lax.rem(lax.div(row_dev, distance), 2) == col_dev, 1, -1)


def listed_bits(cols_ref, count_ref, local_block, own_block, slots):
    bits = jnp.int32(0)
    for s in range(slots):
        bit = lax.shift_left(jnp.int32(1), cols_ref[local_block, s] - own_block + BAND + 1)
        bits = bits | jnp.where(s < count_ref[local_block], bit, 0)
    return bits


def is_listed(bits, offset):
    return (lax.shift_right_logical(bits, offset + BAND + 1) & 1) == 1


def block_offsets(row_dev, col_dev, reach, blocks):
    offsets = [col_dev]
    for d in range(1, reach + 1):
        sign = peer_sign(row_dev, col_dev, d)
        offsets += [sign * (d * blocks) + k for k in range(blocks)]
    return offsets


def weights_kernel(dims, cols_ref, count_ref, own_ref, *rest):
    blocks, size, width, slots, reach, senders = dims
    peers = rest[:reach]
    w_ref, row_ref, col_ref, hl, ee, inv, col_acc, offs = rest[reach:]
    tiles = 1 + reach * blocks
    r, c = lax.axis_index("row"), lax.axis_index("col")
    bits = [listed_bits(cols_ref, count_ref, b, r * blocks + b, slots) for b in range(blocks)]
    for q, offset in enumerate(block_offsets(r, c, reach, blocks)):
        offs[q] = offset

    for b in range(blocks):
        x = own_ref[pl.ds(b * size, size), :].astype(F32)
        scale = lax.rsqrt(jnp.sum(x * x, axis=-1, keepdims=True) * (1.0 / width) + EPS)
        x = x * (scale * (2.0 * KERNEL_SCALE * LOG2E / width))
        high = x.astype(BF16)
        hl[pl.ds(b * size, size), :width] = high
        hl[pl.ds(b * size, size), width:] = (x - high.astype(F32)).astype(BF16)
    ones = jnp.ones((16, 2 * width), BF16)
    for q in range(tiles):
        if q == 0:
            e = own_ref[pl.ds(pl.multiple_of(c * size, size), size), :]
        else:
            e = peers[(q - 1) // blocks][pl.ds((q - 1) % blocks * size, size), :]
        ee[q, :, :width] = e
        ee[q, :, width:] = e
        x = e.astype(F32)
        x = x * x
        high = x.astype(BF16)
        both = jnp.concatenate([high, (x - high.astype(F32)).astype(BF16)], axis=1)
        total = lax.dot_general(ones, both, (((1,), (1,)), ((), ())), preferred_element_type=F32)
        inv[q] = lax.rsqrt(total[:8] * (1.0 / width) + EPS)
    row_ref[...] = jnp.zeros_like(row_ref)
    col_acc[...] = jnp.zeros_like(col_acc)

    def tile(b, q, diagonal):
        s = lax.dot_general(
            hl[pl.ds(pl.multiple_of(b * size, size), size), :],
            ee[q],
            (((1,), (1,)), ((), ())),
            preferred_element_type=F32,
        )
        w = jnp.exp2(s * inv[q, 0:1, :] - 2.0 * KERNEL_SCALE * LOG2E)
        if diagonal:
            ids = lax.broadcasted_iota(jnp.int32, (size, size), 0)
            w = jnp.where(ids == lax.broadcasted_iota(jnp.int32, (size, size), 1), 0.0, w)
        w_ref[b * tiles + q] = w.astype(BF16)
        part = w[:, :LANES]
        for k in range(1, size // LANES):
            part = part + w[:, k * LANES : (k + 1) * LANES]
        row_ref[pl.ds(pl.multiple_of(b * size, size), size), :] += part
        col_acc[q] += jnp.sum(w.reshape(size // 8, 8, size), axis=0)

    tile(c, 0, True)

    @pl.when(is_listed(jnp.where(c == 0, bits[1], bits[0]), 2 * c - 1))
    def _():
        tile(1 - c, 0, False)

    @pl.loop(1, tiles)
    def _(q):
        for b in range(blocks):

            @pl.when(is_listed(bits[b], offs[q] - b))
            def _():
                tile(b, q, False)

    sums = [jnp.sum(col_acc[q], axis=0, keepdims=True) for q in range(tiles)]
    sums += [jnp.zeros((1, size), F32)] * (8 - tiles)
    sums = jnp.concatenate(sums, axis=0).astype(BF16)
    for n in range(senders):
        col_ref[n] = sums


def product_kernel(dims, first, cols_ref, count_ref, *rest):
    blocks, size, width, slots, reach, rows = dims
    tiles = 1 + reach * blocks
    w_ref = rest[0]
    if first:
        sums_ref = rest[1]
        rest = rest[1:]
    own_ref, peers = rest[1], rest[2 : 2 + reach]
    if first:
        out_ref, scale_ref, scaled, scales, offs = rest[2 + reach :]
    else:
        out_ref, offs = rest[2 + reach :]
    r, c = lax.axis_index("row"), lax.axis_index("col")
    bits = [listed_bits(cols_ref, count_ref, b, r * blocks + b, slots) for b in range(blocks)]
    offsets = block_offsets(r, c, reach, blocks)

    if first:
        for n in range(reach + 1):
            chip = r if n == 0 else r + peer_sign(r, c, n) * n
            total = jnp.zeros((blocks, size), F32)
            for shift in range(-reach, reach + 1):
                other, d = chip + shift, abs(shift)
                valid = jnp.logical_and(
                    jnp.logical_and(other >= 0, other < rows), jnp.logical_and(chip >= 0, chip < rows)
                )
                if d == 0:
                    at = jnp.where(valid, other * blocks, 0)
                    term = jnp.concatenate([sums_ref[at + k].astype(F32)[0:1] for k in range(blocks)], axis=0)
                else:
                    core = lax.rem(lax.div(jnp.maximum(chip + min(shift, 0), 0), d), 2)
                    at = jnp.where(valid, other * 2 + core, 0)
                    term = sums_ref[at].astype(F32)[1 + (d - 1) * blocks : 1 + d * blocks]
                total = total + jnp.where(valid, term, 0.0)
            scales[n * blocks : (n + 1) * blocks] = jnp.where(total > 0.0, lax.rsqrt(total), 0.0)
        columns = scales[...].T
        for b in range(blocks):
            scale_ref[pl.ds(b * size, size), :] = jnp.broadcast_to(columns[:, b : b + 1], (size, width))
        s = own_ref[pl.ds(pl.multiple_of(c * size, size), size), :].astype(F32)
        scaled[0] = (s * scale_ref[pl.ds(pl.multiple_of(c * size, size), size), :]).astype(BF16)
        for q in range(1, tiles):
            s = peers[(q - 1) // blocks][pl.ds((q - 1) % blocks * size, size), :].astype(F32)
            scaled[q] = (s * columns[:, blocks + q - 1 : blocks + q]).astype(BF16)
    out_ref[...] = jnp.zeros_like(out_ref)
    for q in range(tiles):
        for b in range(blocks):

            @pl.when(is_listed(bits[b], offsets[q] - b))
            def _():
                if first:
                    s = scaled[q]
                elif q == 0:
                    s = own_ref[pl.ds(pl.multiple_of(c * size, size), size), :]
                else:
                    s = peers[(q - 1) // blocks][pl.ds((q - 1) % blocks * size, size), :]
                out_ref[pl.ds(b * size, size), :] += jnp.dot(
                    w_ref[b * tiles + q], s, preferred_element_type=F32
                )


def row_scale_kernel(own_ref, other_ref, out_ref):
    total = jnp.sum(own_ref[...] + other_ref[...], axis=-1, keepdims=True)
    out_ref[...] = jnp.broadcast_to(ALPHA * lax.rsqrt(total), out_ref.shape)


def state_kernel(own_ref, other_ref, rs_ref, seed_ref, cs_ref, out_ref):
    state = (own_ref[...] + other_ref[...]) * rs_ref[...] + (1.0 - ALPHA) * seed_ref[...]
    out_ref[...] = (state * cs_ref[...]).astype(BF16)


def shards(embeddings, profiles, seed_mask, tile_cols, tile_count):
    rows, cols = lax.axis_size("row"), lax.axis_size("col")
    blocks, slots = tile_cols.shape
    mols, width = embeddings.shape
    prof = profiles.shape[1]
    size = mols // blocks
    reach = (BAND + blocks - 1) // blocks
    tiles = 1 + reach * blocks
    senders = rows * cols
    assert blocks == 2 and cols == 2 and tiles <= 8
    params = pltpu.CompilerParams(vmem_limit_bytes=24 * 1024 * 1024)

    def from_peers(value):
        return [lax.ppermute(value, ("row", "col"), peer_pairs(rows, cols, d)) for d in range(1, reach + 1)]

    def other_core(value):
        return lax.ppermute(value, "col", [(0, 1), (1, 0)])

    peer_emb = from_peers(embeddings)
    seed_rows = seed_mask.astype(F32)[:, None] * profiles
    seeds = seed_rows.astype(BF16)
    peer_seeds = from_peers(seeds)

    weights, row_part, col_part = pl.pallas_call(
        lambda *refs: weights_kernel((blocks, size, width, slots, reach, senders), *refs),
        out_shape=(
            jax.ShapeDtypeStruct((blocks * tiles, size, size), BF16),
            jax.ShapeDtypeStruct((mols, LANES), F32),
            jax.ShapeDtypeStruct((senders, 8, size), BF16),
        ),
        in_specs=[SMEM, SMEM] + [VMEM] * (1 + reach),
        out_specs=(VMEM, VMEM, VMEM),
        scratch_shapes=[
            pltpu.VMEM((mols, 2 * width), BF16),
            pltpu.VMEM((tiles, size, 2 * width), BF16),
            pltpu.VMEM((tiles, 8, size), F32),
            pltpu.VMEM((tiles, 8, size), F32),
            pltpu.SMEM((tiles,), jnp.int32),
        ],
        compiler_params=params,
        name="weights",
    )(tile_cols, tile_count, embeddings, *peer_emb)

    col_sums = lax.all_to_all(col_part, ("row", "col"), 0, 0, tiled=True)
    row_scale = pl.pallas_call(
        row_scale_kernel,
        out_shape=jax.ShapeDtypeStruct((mols, LANES), F32),
        in_specs=[VMEM, VMEM],
        out_specs=VMEM,
        compiler_params=params,
        name="row_scale",
    )(row_part, other_core(row_part))

    dims = (blocks, size, prof, slots, reach, rows)
    partial, col_scale = pl.pallas_call(
        lambda *refs: product_kernel(dims, True, *refs),
        out_shape=(jax.ShapeDtypeStruct((mols, prof), F32), jax.ShapeDtypeStruct((mols, prof), F32)),
        in_specs=[SMEM, SMEM] + [VMEM] * (3 + reach),
        out_specs=(VMEM, VMEM),
        scratch_shapes=[
            pltpu.VMEM((tiles, size, prof), BF16),
            pltpu.VMEM((8, size), F32),
            pltpu.SMEM((tiles,), jnp.int32),
        ],
        compiler_params=params,
        name="first_product",
    )(tile_cols, tile_count, weights, col_sums, seeds, *peer_seeds)

    for iteration in range(1, ITERS):
        scaled = pl.pallas_call(
            state_kernel,
            out_shape=jax.ShapeDtypeStruct((mols, prof), BF16),
            in_specs=[VMEM] * 5,
            out_specs=VMEM,
            compiler_params=params,
            name="state",
        )(partial, other_core(partial), row_scale, seed_rows, col_scale)
        partial = pl.pallas_call(
            lambda *refs: product_kernel(dims, False, *refs),
            out_shape=jax.ShapeDtypeStruct((mols, prof), F32),
            in_specs=[SMEM, SMEM] + [VMEM] * (2 + reach),
            out_specs=VMEM,
            scratch_shapes=[pltpu.SMEM((tiles,), jnp.int32)],
            compiler_params=params,
            name="product",
        )(tile_cols, tile_count, weights, scaled, *from_peers(scaled))
    return (partial + other_core(partial)) * row_scale + (1.0 - ALPHA) * seed_rows


def solution(mesh):
    placed = (
        P(("grp", "row"), None),
        P(("grp", "row"), None),
        P(("grp", "row")),
        P(("grp", "row"), None),
        P(("grp", "row")),
    )
    return jax.shard_map(
        shards, mesh=mesh, in_specs=placed, out_specs=P(("grp", "row"), None), check_vma=False
    )
```

```python
import jax
import jax.numpy as jnp
from jax import lax
from jax.experimental import pallas as pl
from jax.experimental.pallas import tpu as pltpu
from jax.sharding import PartitionSpec as P

BAND = 6
ITERS = 2

KERNEL_SCALE = 12.5
ALPHA = 0.8
EPS = 1e-06
LOG2E = 1.4426950408889634
LANES = 128
F32 = jnp.float32
BF16 = jnp.bfloat16

VMEM = pl.BlockSpec(memory_space=pltpu.VMEM)
HBM = pl.BlockSpec(memory_space=pltpu.HBM)


def peer_pairs(rows, cols, distance):
    pairs = []
    for low in range(rows - distance):
        core = (low // distance) % cols
        a, b = low * cols + core, (low + distance) * cols + core
        pairs += [(a, b), (b, a)]
    return pairs


def peer_sign(row_dev, col_dev, distance):
    return jnp.where(lax.rem(lax.div(row_dev, distance), 2) == col_dev, 1, -1)


def listed_bits(cols_ref, count_ref, local_block, own_block, slots):
    bits = jnp.int32(0)
    for s in range(slots):
        bit = lax.shift_left(jnp.int32(1), cols_ref[local_block, s] - own_block + BAND + 1)
        bits = bits | jnp.where(s < count_ref[local_block], bit, 0)
    return bits


def is_listed(bits, offset):
    return (lax.shift_right_logical(bits, offset + BAND + 1) & 1) == 1


def block_offsets(row_dev, col_dev, reach, blocks):
    offsets = [col_dev]
    for d in range(1, reach + 1):
        sign = peer_sign(row_dev, col_dev, d)
        offsets += [sign * (d * blocks) + k for k in range(blocks)]
    return offsets


def weights_kernel(dims, cols_hbm, count_hbm, own_hbm, *rest):
    blocks, size, width, slots, reach, senders = dims
    peers = rest[:reach]
    w_hbm, row_ref, col_ref, w_ref, own_ref, hl, ee, inv, col_acc, offs, cols_ref, count_ref, sems, w_sems = rest[reach:]
    tiles = 1 + reach * blocks
    r, c = lax.axis_index("row"), lax.axis_index("col")
    loads = [
        pltpu.make_async_copy(own_hbm, own_ref, sems.at[0]),
        pltpu.make_async_copy(cols_hbm, cols_ref, sems.at[1]),
        pltpu.make_async_copy(count_hbm, count_ref, sems.at[2]),
    ]
    for load in loads:
        load.start()
    for q, offset in enumerate(block_offsets(r, c, reach, blocks)):
        offs[q] = offset

    ones = jnp.ones((16, 2 * width), BF16)

    def column_side(q, e):
        ee[q, :, :width] = e
        ee[q, :, width:] = e
        x = e.astype(F32)
        x = x * x
        high = x.astype(BF16)
        both = jnp.concatenate([high, (x - high.astype(F32)).astype(BF16)], axis=1)
        total = lax.dot_general(ones, both, (((1,), (1,)), ((), ())), preferred_element_type=F32)
        inv[q] = lax.rsqrt(total[:8] * (1.0 / width) + EPS)

    for q in range(1, tiles):
        column_side(q, peers[(q - 1) // blocks][pl.ds((q - 1) % blocks * size, size), :])
    row_ref[...] = jnp.zeros_like(row_ref)
    col_acc[...] = jnp.zeros_like(col_acc)
    for load in loads:
        load.wait()
    bits = [listed_bits(cols_ref, count_ref, b, r * blocks + b, slots) for b in range(blocks)]
    column_side(0, own_ref[pl.ds(pl.multiple_of(c * size, size), size), :])
    for b in range(blocks):
        x = own_ref[pl.ds(b * size, size), :].astype(F32)
        scale = lax.rsqrt(jnp.sum(x * x, axis=-1, keepdims=True) * (1.0 / width) + EPS)
        x = x * (scale * (2.0 * KERNEL_SCALE * LOG2E / width))
        high = x.astype(BF16)
        hl[pl.ds(b * size, size), :width] = high
        hl[pl.ds(b * size, size), width:] = (x - high.astype(F32)).astype(BF16)
    def store(b, q):
        at = b * tiles + q
        return pltpu.make_async_copy(w_ref.at[at], w_hbm.at[at], w_sems.at[at])

    def tile(b, q, diagonal):
        s = lax.dot_general(
            hl[pl.ds(pl.multiple_of(b * size, size), size), :],
            ee[q],
            (((1,), (1,)), ((), ())),
            preferred_element_type=F32,
        )
        w = jnp.exp2(s * inv[q, 0:1, :] - 2.0 * KERNEL_SCALE * LOG2E)
        if diagonal:
            ids = lax.broadcasted_iota(jnp.int32, (size, size), 0)
            w = jnp.where(ids == lax.broadcasted_iota(jnp.int32, (size, size), 1), 0.0, w)
        w_ref[b * tiles + q] = w.astype(BF16)
        store(b, q).start()
        part = w[:, :LANES]
        for k in range(1, size // LANES):
            part = part + w[:, k * LANES : (k + 1) * LANES]
        row_ref[pl.ds(pl.multiple_of(b * size, size), size), :] += part
        col_acc[q] += jnp.sum(w.reshape(size // 8, 8, size), axis=0)

    tile(c, 0, True)

    @pl.when(is_listed(jnp.where(c == 0, bits[1], bits[0]), 2 * c - 1))
    def _():
        tile(1 - c, 0, False)

    @pl.loop(1, tiles)
    def _(q):
        for b in range(blocks):

            @pl.when(is_listed(bits[b], offs[q] - b))
            def _():
                tile(b, q, False)

    sums = [jnp.sum(col_acc[q], axis=0, keepdims=True) for q in range(tiles)]
    sums += [jnp.zeros((1, size), F32)] * (8 - tiles)
    sums = jnp.concatenate(sums, axis=0).astype(BF16)
    for n in range(senders):
        col_ref[n] = sums
    for q in range(tiles):
        for b in range(blocks):

            @pl.when(is_listed(bits[b], offs[q] - b))
            def _():
                store(b, q).wait()


def product_kernel(dims, first, cols_hbm, count_hbm, w_src, *rest):
    blocks, size, width, slots, reach, rows = dims
    tiles = 1 + reach * blocks
    if first:
        sums_ref, rest = rest[0], rest[1:]
    own_ref, peers = rest[0], rest[1 : 1 + reach]
    if first:
        out_ref, scale_ref, w_ref, scaled, scales, cols_ref, count_ref, sems, w_sems = rest[1 + reach :]
    else:
        out_ref, cols_ref, count_ref, sems = rest[1 + reach :]
        w_ref = w_src
    r, c = lax.axis_index("row"), lax.axis_index("col")
    loads = [
        pltpu.make_async_copy(cols_hbm, cols_ref, sems.at[0]),
        pltpu.make_async_copy(count_hbm, count_ref, sems.at[1]),
    ]
    for load in loads:
        load.start()
    offsets = block_offsets(r, c, reach, blocks)
    out_ref[...] = jnp.zeros_like(out_ref)
    for load in loads:
        load.wait()
    bits = [listed_bits(cols_ref, count_ref, b, r * blocks + b, slots) for b in range(blocks)]

    def fetch(b, q):
        at = b * tiles + q
        return pltpu.make_async_copy(w_src.at[at], w_ref.at[at], w_sems.at[at])

    if first:
        for q in range(tiles):
            for b in range(blocks):

                @pl.when(is_listed(bits[b], offsets[q] - b))
                def _():
                    fetch(b, q).start()

    if first:
        for n in range(reach + 1):
            chip = r if n == 0 else r + peer_sign(r, c, n) * n
            total = jnp.zeros((blocks, size), F32)
            for shift in range(-reach, reach + 1):
                other, d = chip + shift, abs(shift)
                valid = jnp.logical_and(
                    jnp.logical_and(other >= 0, other < rows), jnp.logical_and(chip >= 0, chip < rows)
                )
                if d == 0:
                    at = jnp.where(valid, other * blocks, 0)
                    term = jnp.concatenate([sums_ref[at + k].astype(F32)[0:1] for k in range(blocks)], axis=0)
                else:
                    core = lax.rem(lax.div(jnp.maximum(chip + min(shift, 0), 0), d), 2)
                    at = jnp.where(valid, other * 2 + core, 0)
                    term = sums_ref[at].astype(F32)[1 + (d - 1) * blocks : 1 + d * blocks]
                total = total + jnp.where(valid, term, 0.0)
            scales[n * blocks : (n + 1) * blocks] = jnp.where(total > 0.0, lax.rsqrt(total), 0.0)
        columns = scales[...].T
        for b in range(blocks):
            scale_ref[pl.ds(b * size, size), :] = jnp.broadcast_to(columns[:, b : b + 1], (size, width))
        s = own_ref[pl.ds(pl.multiple_of(c * size, size), size), :].astype(F32)
        scaled[0] = (s * scale_ref[pl.ds(pl.multiple_of(c * size, size), size), :]).astype(BF16)
        for q in range(1, tiles):
            s = peers[(q - 1) // blocks][pl.ds((q - 1) % blocks * size, size), :].astype(F32)
            scaled[q] = (s * columns[:, blocks + q - 1 : blocks + q]).astype(BF16)
    for q in range(tiles):
        for b in range(blocks):

            @pl.when(is_listed(bits[b], offsets[q] - b))
            def _():
                if first:
                    fetch(b, q).wait()
                    s = scaled[q]
                elif q == 0:
                    s = own_ref[pl.ds(pl.multiple_of(c * size, size), size), :]
                else:
                    s = peers[(q - 1) // blocks][pl.ds((q - 1) % blocks * size, size), :]
                out_ref[pl.ds(b * size, size), :] += jnp.dot(
                    w_ref[b * tiles + q], s, preferred_element_type=F32
                )


def row_scale_kernel(own_ref, other_ref, out_ref):
    total = jnp.sum(own_ref[...] + other_ref[...], axis=-1, keepdims=True)
    out_ref[...] = jnp.broadcast_to(ALPHA * lax.rsqrt(total), out_ref.shape)


def state_kernel(own_ref, other_ref, rs_ref, seed_ref, cs_ref, out_ref):
    state = (own_ref[...] + other_ref[...]) * rs_ref[...] + (1.0 - ALPHA) * seed_ref[...]
    out_ref[...] = (state * cs_ref[...]).astype(BF16)


def shards(embeddings, profiles, seed_mask, tile_cols, tile_count):
    rows, cols = lax.axis_size("row"), lax.axis_size("col")
    blocks, slots = tile_cols.shape
    mols, width = embeddings.shape
    prof = profiles.shape[1]
    size = mols // blocks
    reach = (BAND + blocks - 1) // blocks
    tiles = 1 + reach * blocks
    senders = rows * cols
    assert blocks == 2 and cols == 2 and tiles <= 8
    params = pltpu.CompilerParams(vmem_limit_bytes=24 * 1024 * 1024)

    tables = [pltpu.SMEM(tile_cols.shape, jnp.int32), pltpu.SMEM(tile_count.shape, jnp.int32)]

    def from_peers(value):
        return [lax.ppermute(value, ("row", "col"), peer_pairs(rows, cols, d)) for d in range(1, reach + 1)]

    def other_core(value):
        return lax.ppermute(value, "col", [(0, 1), (1, 0)])

    peer_emb = from_peers(embeddings)
    tables_hbm = [pltpu.with_memory_space_constraint(t, pltpu.HBM) for t in (tile_cols, tile_count)]
    emb_hbm = pltpu.with_memory_space_constraint(embeddings, pltpu.HBM)
    seed_rows = jnp.where(seed_mask[:, None] > 0, profiles, 0.0)
    seeds = seed_rows.astype(BF16)
    peer_seeds = from_peers(seeds)

    weights, row_part, col_part = pl.pallas_call(
        lambda *refs: weights_kernel((blocks, size, width, slots, reach, senders), *refs),
        out_shape=(
            pltpu.HBM((blocks * tiles, size, size), BF16),
            jax.ShapeDtypeStruct((mols, LANES), F32),
            jax.ShapeDtypeStruct((senders, 8, size), BF16),
        ),
        in_specs=[HBM] * 3 + [VMEM] * reach,
        out_specs=(HBM, VMEM, VMEM),
        scratch_shapes=[
            pltpu.VMEM((blocks * tiles, size, size), BF16),
            pltpu.VMEM((mols, width), BF16),
            pltpu.VMEM((mols, 2 * width), BF16),
            pltpu.VMEM((tiles, size, 2 * width), BF16),
            pltpu.VMEM((tiles, 8, size), F32),
            pltpu.VMEM((tiles, 8, size), F32),
            pltpu.SMEM((tiles,), jnp.int32),
            *tables,
            pltpu.SemaphoreType.DMA((3,)),
            pltpu.SemaphoreType.DMA((blocks * tiles,)),
        ],
        compiler_params=params,
        name="weights",
    )(*tables_hbm, emb_hbm, *peer_emb)

    col_sums = lax.all_to_all(col_part, ("row", "col"), 0, 0, tiled=True)
    row_scale = pl.pallas_call(
        row_scale_kernel,
        out_shape=jax.ShapeDtypeStruct((mols, LANES), F32),
        in_specs=[VMEM, VMEM],
        out_specs=VMEM,
        compiler_params=params,
        name="row_scale",
    )(row_part, other_core(row_part))

    dims = (blocks, size, prof, slots, reach, rows)
    partial, col_scale, weights = pl.pallas_call(
        lambda *refs: product_kernel(dims, True, *refs),
        out_shape=(
            jax.ShapeDtypeStruct((mols, prof), F32),
            jax.ShapeDtypeStruct((mols, prof), F32),
            jax.ShapeDtypeStruct((blocks * tiles, size, size), BF16),
        ),
        in_specs=[HBM] * 3 + [VMEM] * (2 + reach),
        out_specs=(VMEM, VMEM, VMEM),
        scratch_shapes=[
            pltpu.VMEM((tiles, size, prof), BF16),
            pltpu.VMEM((8, size), F32),
            *tables,
            pltpu.SemaphoreType.DMA((2,)),
            pltpu.SemaphoreType.DMA((blocks * tiles,)),
        ],
        compiler_params=params,
        name="first_product",
    )(*tables_hbm, pltpu.with_memory_space_constraint(weights, pltpu.HBM), col_sums, seeds, *peer_seeds)

    for iteration in range(1, ITERS):
        scaled = pl.pallas_call(
            state_kernel,
            out_shape=jax.ShapeDtypeStruct((mols, prof), BF16),
            in_specs=[VMEM] * 5,
            out_specs=VMEM,
            compiler_params=params,
            name="state",
        )(partial, other_core(partial), row_scale, seed_rows, col_scale)
        partial = pl.pallas_call(
            lambda *refs: product_kernel(dims, False, *refs),
            out_shape=jax.ShapeDtypeStruct((mols, prof), F32),
            in_specs=[HBM] * 2 + [VMEM] * (2 + reach),
            out_specs=VMEM,
            scratch_shapes=[*tables, pltpu.SemaphoreType.DMA((2,))],
            compiler_params=params,
            name="product",
        )(*tables_hbm, weights, scaled, *from_peers(scaled))
    return (partial + other_core(partial)) * row_scale + (1.0 - ALPHA) * seed_rows


def solution(mesh):
    placed = (
        P(("grp", "row"), None),
        P(("grp", "row"), None),
        P(("grp", "row")),
        P(("grp", "row"), None),
        P(("grp", "row")),
    )
    return jax.shard_map(
        shards, mesh=mesh, in_specs=placed, out_specs=P(("grp", "row"), None), check_vma=False
    )
```

```python
import jax
import jax.numpy as jnp
from jax import lax
from jax.experimental import pallas as pl
from jax.experimental.pallas import tpu as pltpu
from jax.sharding import PartitionSpec as P

BAND = 6
ITERS = 2

KERNEL_SCALE = 12.5
ALPHA = 0.8
EPS = 1e-06
LOG2E = 1.4426950408889634
LANES = 128
TAIL = 16
F32 = jnp.float32
BF16 = jnp.bfloat16

VMEM = pl.BlockSpec(memory_space=pltpu.VMEM)
HBM = pl.BlockSpec(memory_space=pltpu.HBM)
PARAMS = pltpu.CompilerParams(vmem_limit_bytes=24 * 1024 * 1024)


def peer_pairs(rows, cols, distance):
    pairs = []
    for low in range(rows - distance):
        core = (low // distance) % cols
        a, b = low * cols + core, (low + distance) * cols + core
        pairs += [(a, b), (b, a)]
    busy = {a for a, _ in pairs}
    idle = [n for n in range(rows * cols) if n not in busy]
    for a, b in zip(idle[::2], idle[1::2]):
        pairs += [(a, b), (b, a)]
    return pairs


def peer_sign(distance):
    return jnp.where(lax.rem(lax.div(lax.axis_index("row"), distance), 2) == lax.axis_index("col"), 1, -1)


def table_entry(table, row, offset):
    lane = lax.broadcasted_iota(jnp.int32, (1, LANES), 1)
    return jnp.max(jnp.where(lane == offset + BAND, table[row : row + 1, :], 0.0), axis=-1, keepdims=True)


def lanes_sum(w):
    part = w[:, :LANES]
    for k in range(1, w.shape[1] // LANES):
        part = part + w[:, k * LANES : (k + 1) * LANES]
    return part


def pack_kernel(blocks, slots, emb_hbm, cols_hbm, count_hbm, out_ref, cols_ref, count_ref, sems):
    mols = emb_hbm.shape[0]
    loads = [
        pltpu.make_async_copy(emb_hbm, out_ref.at[pl.ds(0, mols), :], sems.at[0]),
        pltpu.make_async_copy(cols_hbm, cols_ref, sems.at[1]),
        pltpu.make_async_copy(count_hbm, count_ref, sems.at[2]),
    ]
    for load in loads:
        load.start()
    loads[1].wait()
    loads[2].wait()
    first = lax.axis_index("row") * blocks
    lane = lax.broadcasted_iota(jnp.int32, (TAIL, LANES), 1)
    row = lax.broadcasted_iota(jnp.int32, (TAIL, LANES), 0)
    table = jnp.zeros((TAIL, LANES), F32)
    for b in range(blocks):
        for s in range(slots):
            offset = jnp.where(s < count_ref[b], cols_ref[b, s] - (first + b) + BAND, -1)
            table = jnp.where(jnp.logical_and(lane == offset, row == b), 1.0, table)
    out_ref[pl.ds(mols, TAIL), :] = table.astype(BF16)
    loads[0].wait()


def tile_weights(hl, b, e, w_ref, at, s_ref, diagonal):
    size, width = e.shape
    x = e.astype(F32)
    x = x * x
    high = x.astype(BF16)
    both = jnp.concatenate([high, (x - high.astype(F32)).astype(BF16)], axis=1)
    nt = (((1,), (1,)), ((), ()))
    total = lax.dot_general(jnp.ones((TAIL, 2 * width), BF16), both, nt, preferred_element_type=F32)
    inv = lax.rsqrt(total[0:1] * (1.0 / width) + EPS)
    ee = jnp.concatenate([e, e], axis=1)
    s_ref[...] = lax.dot_general(hl[pl.ds(b * size, size), :], ee, nt, preferred_element_type=F32)
    parts = []
    rows = 32
    for k in range(size // rows):
        w = jnp.exp2(s_ref[pl.ds(k * rows, rows), :] * inv - 2.0 * KERNEL_SCALE * LOG2E)
        if diagonal is not None:
            i = lax.broadcasted_iota(jnp.int32, (rows, size), 0) + k * rows
            j = lax.broadcasted_iota(jnp.int32, (rows, size), 1)
            w = jnp.where(jnp.logical_and(i == j, diagonal), 0.0, w)
        w_ref[at, pl.ds(k * rows, rows), :] = w.astype(BF16)
        parts.append(lanes_sum(w))
    return parts


def add_parts(ref, first, parts, mask, start):
    rows = parts[0].shape[0]
    for k, part in enumerate(parts):
        at = pl.ds(first + k * rows, rows)
        value = part * mask
        ref[at, :] = value if start else ref[at, :] + value


def own_weights_kernel(blocks, pack_ref, hl, w_ref, row_ref, col_ref, s_ref):
    mols = hl.shape[0]
    size, width = mols // blocks, hl.shape[1] // 2
    c = lax.axis_index("col")
    table = pack_ref[pl.ds(mols, TAIL), :].astype(F32)
    for b in range(blocks):
        x = pack_ref[pl.ds(b * size, size), :].astype(F32)
        scale = lax.rsqrt(jnp.sum(x * x, axis=-1, keepdims=True) * (1.0 / width) + EPS)
        x = x * (scale * (2.0 * KERNEL_SCALE * LOG2E / width))
        high = x.astype(BF16)
        hl[pl.ds(b * size, size), :width] = high
        hl[pl.ds(b * size, size), width:] = (x - high.astype(F32)).astype(BF16)
    e = pack_ref[pl.ds(pl.multiple_of(c * size, size), size), :]
    for b in range(blocks):
        parts = tile_weights(hl, b, e, w_ref, b, s_ref, c == b)
        from_c = jnp.where(c == 0, table_entry(table, 0, b), table_entry(table, 1, b - 1))
        add_parts(row_ref, b * size, parts, table_entry(table, b, c - b), True)
        add_parts(col_ref, b * size, parts, from_c, True)


def peer_weights_kernel(dims, distance, pack_ref, peer_ref, hl, row_in, col_in, w_ref, *rest):
    blocks, rows, last = dims
    if last:
        deg_ref, row_ref, col_ref, s_ref = rest
    else:
        row_ref, col_ref, s_ref = rest
    mols = hl.shape[0]
    size = mols // blocks
    sign = peer_sign(distance)
    peer = lax.axis_index("row") + sign * distance
    valid = jnp.where(jnp.logical_and(peer >= 0, peer < rows), 1.0, 0.0)
    own_table = pack_ref[pl.ds(mols, TAIL), :].astype(F32)
    peer_table = peer_ref[pl.ds(mols, TAIL), :].astype(F32) * valid
    row_ref[...] = row_in[...]
    col_ref[...] = col_in[...]
    for k in range(blocks):
        e = peer_ref[pl.ds(k * size, size), :]
        for b in range(blocks):
            offset = sign * (distance * blocks) + (k - b)
            parts = tile_weights(hl, b, e, w_ref, k * blocks + b, s_ref, None)
            add_parts(row_ref, b * size, parts, table_entry(own_table, b, offset), False)
            add_parts(col_ref, b * size, parts, table_entry(peer_table, k, -offset), False)
    if last:
        lane = lax.broadcasted_iota(jnp.int32, (size, LANES), 1)
        for b in range(blocks):
            at = pl.ds(b * size, size)
            by_row = jnp.sum(row_ref[at, :], axis=-1, keepdims=True)
            by_col = jnp.sum(col_ref[at, :], axis=-1, keepdims=True)
            deg_ref[at, :] = jnp.where(lane < LANES // 2, by_row, by_col)


def scale_kernel(own_ref, other_ref, seed_ref, scaled_ref, rs_ref, cs_ref):
    total = lax.rsqrt(own_ref[...] + other_ref[...])
    by_col = jnp.broadcast_to(total[:, LANES // 2 : LANES // 2 + 1], total.shape)
    rs_ref[...] = jnp.broadcast_to(total[:, 0:1] * ALPHA, total.shape)
    cs_ref[...] = by_col
    scaled_ref[...] = (seed_ref[...] * by_col).astype(BF16)


def product_kernel(blocks, distance, pack_ref, w_ref, scaled_ref, *rest):
    out_ref = rest[-1]
    mols = scaled_ref.shape[0]
    size = mols // blocks
    table = pack_ref[pl.ds(mols, TAIL), :].astype(F32)
    c = lax.axis_index("col")
    for b in range(blocks):
        at = pl.ds(b * size, size)
        if distance == 0:
            s = scaled_ref[pl.ds(pl.multiple_of(c * size, size), size), :].astype(F32)
            s = (s * table_entry(table, b, c - b)).astype(BF16)
            out_ref[at, :] = jnp.dot(w_ref[b], s, preferred_element_type=F32)
            continue
        total = rest[0][at, :]
        for k in range(blocks):
            offset = peer_sign(distance) * (distance * blocks) + (k - b)
            s = scaled_ref[pl.ds(k * size, size), :].astype(F32)
            s = (s * table_entry(table, b, offset)).astype(BF16)
            total = total + jnp.dot(w_ref[k * blocks + b], s, preferred_element_type=F32)
        out_ref[at, :] = total


def state_kernel(own_ref, other_ref, rs_ref, seed_ref, cs_ref, out_ref):
    state = (own_ref[...] + other_ref[...]) * rs_ref[...] + (1.0 - ALPHA) * seed_ref[...]
    out_ref[...] = (state * cs_ref[...]).astype(BF16)


def kernel_call(body, name, ins, outs, flops, scratch=(), in_specs=None):
    return pl.pallas_call(
        body,
        out_shape=outs,
        in_specs=in_specs or [VMEM] * len(ins),
        out_specs=jax.tree.map(lambda _: VMEM, outs),
        scratch_shapes=scratch,
        compiler_params=PARAMS,
        cost_estimate=pl.CostEstimate(flops=flops, bytes_accessed=1 << 20, transcendentals=0),
        name=name,
    )(*ins)


def shards(embeddings, profiles, seed_mask, tile_cols, tile_count):
    rows, cols = lax.axis_size("row"), lax.axis_size("col")
    blocks, slots = tile_cols.shape
    mols, width = embeddings.shape
    prof = profiles.shape[1]
    size = mols // blocks
    reach = (BAND + blocks - 1) // blocks
    assert blocks == 2 and cols == 2 and width == LANES and prof == LANES
    f32_rows = jax.ShapeDtypeStruct((mols, LANES), F32)
    bf16_rows = jax.ShapeDtypeStruct((mols, LANES), BF16)
    tile_flops = 4 * size * size * width

    def from_peers(value):
        return [lax.ppermute(value, ("row", "col"), peer_pairs(rows, cols, d)) for d in range(1, reach + 1)]

    def other_core(value):
        return lax.ppermute(value, "col", [(0, 1), (1, 0)])

    def weights_of(tiles):
        return jax.ShapeDtypeStruct((tiles, size, size), BF16)

    held = [pltpu.with_memory_space_constraint(t, pltpu.HBM) for t in (embeddings, tile_cols, tile_count)]
    pack = kernel_call(
        lambda *refs: pack_kernel(blocks, slots, *refs),
        "pack",
        held,
        jax.ShapeDtypeStruct((mols + TAIL, LANES), BF16),
        1,
        [
            pltpu.SMEM(tile_cols.shape, jnp.int32),
            pltpu.SMEM(tile_count.shape, jnp.int32),
            pltpu.SemaphoreType.DMA((3,)),
        ],
        [HBM] * 3,
    )
    peer_packs = from_peers(pack)
    seed_rows = jnp.where(seed_mask[:, None] > 0, profiles, 0.0)
    one_tile = pltpu.VMEM((size, size), F32)
    hl, own_weights, row_sum, col_sum = kernel_call(
        lambda *refs: own_weights_kernel(blocks, *refs),
        "own_weights",
        [pack],
        (jax.ShapeDtypeStruct((mols, 2 * width), BF16), weights_of(blocks), f32_rows, f32_rows),
        blocks * tile_flops,
        [one_tile],
    )
    weights = [own_weights]
    for d in range(1, reach + 1):
        last = d == reach
        ins = [pack, peer_packs[d - 1], hl, row_sum, col_sum]
        out = kernel_call(
            lambda *refs, d=d, last=last: peer_weights_kernel((blocks, rows, last), d, *refs),
            "peer_weights",
            ins,
            (weights_of(blocks * blocks), f32_rows) if last else (weights_of(blocks * blocks), f32_rows, f32_rows),
            blocks * blocks * tile_flops,
            [pltpu.VMEM((mols, LANES), F32)] * 2 + [one_tile] if last else [one_tile],
        )
        weights.append(out[0])
        if last:
            degree = out[1]
        else:
            row_sum, col_sum = out[1:]
    scaled, row_scale, col_scale = kernel_call(
        scale_kernel, "scale", [degree, other_core(degree), seed_rows], (bf16_rows, f32_rows, f32_rows), 1
    )
    for iteration in range(ITERS):
        peers = from_peers(scaled)
        partial = kernel_call(
            lambda *refs: product_kernel(blocks, 0, *refs),
            "own_product",
            [pack, weights[0], scaled],
            f32_rows,
            blocks * tile_flops,
        )
        for d in range(1, reach + 1):
            partial = kernel_call(
                lambda *refs, d=d: product_kernel(blocks, d, *refs),
                "peer_product",
                [pack, weights[d], peers[d - 1], partial],
                f32_rows,
                blocks * blocks * tile_flops,
            )
        other = other_core(partial)
        if iteration + 1 < ITERS:
            scaled = kernel_call(
                state_kernel, "state", [partial, other, row_scale, seed_rows, col_scale], bf16_rows, 1
            )
    return (partial + other) * row_scale + (1.0 - ALPHA) * seed_rows


def solution(mesh):
    placed = (
        P(("grp", "row"), None),
        P(("grp", "row"), None),
        P(("grp", "row")),
        P(("grp", "row"), None),
        P(("grp", "row")),
    )
    return jax.shard_map(
        shards, mesh=mesh, in_specs=placed, out_specs=P(("grp", "row"), None), check_vma=False
    )
```

```python
import itertools

import jax
import jax.numpy as jnp
from jax import lax
from jax.experimental import pallas as pl
from jax.experimental.pallas import tpu as pltpu
from jax.sharding import PartitionSpec as P

BAND = 6
ITERS = 2

KERNEL_SCALE = 12.5
ALPHA = 0.8
EPS = 1e-06
LOG2E = 1.4426950408889634
LANES = 128
TAIL = 16
F32 = jnp.float32
BF16 = jnp.bfloat16

VMEM = pl.BlockSpec(memory_space=pltpu.VMEM)
HBM = pl.BlockSpec(memory_space=pltpu.HBM)
PARAMS = pltpu.CompilerParams(vmem_limit_bytes=24 * 1024 * 1024)


def search_steps(rows, reach):
    if reach != 3 or rows < 8:
        return None
    edges = [(a, a + d) for a in range(rows) for d in range(1, reach + 1) if a + d < rows]

    def solve(room):
        chosen = []

        def place(n):
            done = edges[n][0] if n < len(edges) else rows
            if any(room[chip][step] for chip in range(max(done - reach, 0), done) for step in range(reach)):
                return False
            if n == len(edges):
                return True
            a, b = edges[n]
            for k in range(reach):
                step = (b - a - 1 + k) % reach
                if room[a][step] and room[b][step]:
                    room[a][step] -= 1
                    room[b][step] -= 1
                    chosen.append(step)
                    if place(n + 1):
                        return True
                    room[a][step] += 1
                    room[b][step] += 1
                    chosen.pop()
            return False

        return chosen if place(0) else None

    best, best_moved = None, None
    orders = list(itertools.permutations(range(reach)))
    for low, near_low, high, near_high in itertools.product(orders, range(reach), orders, range(reach)):
        room = [[2] * reach for _ in range(rows)]
        for chip, way, order, near in ((0, 1, low, near_low), (rows - 1, -1, high, near_high)):
            for k in range(reach):
                room[chip][order[k]] = k
            room[chip + way][near] = 0
            room[chip + 2 * way][order[1]] = 1
        chosen = solve(room)
        if chosen is not None:
            moved = sum(step != b - a - 1 for (a, b), step in zip(edges, chosen))
            if best is None or moved < best_moved:
                best, best_moved = chosen, moved
    if best is None:
        return None
    return [[e for e, s in zip(edges, best) if s == step] for step in range(reach)]


def swap_steps(rows, cols, reach):
    chip_steps = search_steps(rows, reach)
    if chip_steps is None:
        chip_steps = [[(a, a + d) for a in range(rows - d)] for d in range(1, reach + 1)]
    steps = []
    for chip_pairs in chip_steps:
        free = [list(range(cols)) for _ in range(rows)]
        offsets = [[0] * rows for _ in range(cols)]
        swaps = []
        for a, b in chip_pairs:
            core_a, core_b = free[a].pop(0), free[b].pop(0)
            swaps.append((a * cols + core_a, b * cols + core_b))
            offsets[core_a][a], offsets[core_b][b] = b - a, a - b
        idle = []
        for chip, cores in enumerate(free):
            if len(cores) == 2:
                swaps.append((chip * cols + cores[0], chip * cols + cores[1]))
            else:
                idle += [chip * cols + core for core in cores]
        swaps += list(zip(idle[::2], idle[1::2]))
        steps.append((swaps + [(b, a) for a, b in swaps], offsets))
    return steps


def peer_offset(offsets):
    r, c = lax.axis_index("row"), lax.axis_index("col")
    value = jnp.int32(0)
    for core, per_row in enumerate(offsets):
        for word, first in enumerate(range(0, len(per_row), 8)):
            code = sum((offset + 8) << (4 * n) for n, offset in enumerate(per_row[first : first + 8]))
            code = jnp.int32(code - (1 << 32) if code >= 1 << 31 else code)
            digit = (lax.shift_right_logical(code, 4 * lax.rem(r, 8)) & 15) - 8
            here = jnp.logical_and(c == core, lax.div(r, 8) == word)
            value = jnp.where(here, digit, value)
    return value


def table_entry(table, row, offset):
    lane = lax.broadcasted_iota(jnp.int32, (1, LANES), 1)
    return jnp.max(jnp.where(lane == offset + BAND, table[row : row + 1, :], 0.0), axis=-1, keepdims=True)


def lanes_sum(w):
    part = w[:, :LANES]
    for k in range(1, w.shape[1] // LANES):
        part = part + w[:, k * LANES : (k + 1) * LANES]
    return part


def pack_kernel(blocks, slots, emb_hbm, cols_hbm, count_hbm, out_ref, cols_ref, count_ref, sems):
    mols = emb_hbm.shape[0]
    loads = [
        pltpu.make_async_copy(emb_hbm, out_ref.at[pl.ds(0, mols), :], sems.at[0]),
        pltpu.make_async_copy(cols_hbm, cols_ref, sems.at[1]),
        pltpu.make_async_copy(count_hbm, count_ref, sems.at[2]),
    ]
    for load in loads:
        load.start()
    loads[1].wait()
    loads[2].wait()
    first = lax.axis_index("row") * blocks
    lane = lax.broadcasted_iota(jnp.int32, (TAIL, LANES), 1)
    row = lax.broadcasted_iota(jnp.int32, (TAIL, LANES), 0)
    table = jnp.zeros((TAIL, LANES), F32)
    for b in range(blocks):
        for s in range(slots):
            offset = jnp.where(s < count_ref[b], cols_ref[b, s] - (first + b) + BAND, -1)
            table = jnp.where(jnp.logical_and(lane == offset, row == b), 1.0, table)
    out_ref[pl.ds(mols, TAIL), :] = table.astype(BF16)
    loads[0].wait()


def tile_weights(hl, b, e, w_ref, at, s_ref, diagonal):
    size, width = e.shape
    x = e.astype(F32)
    x = x * x
    high = x.astype(BF16)
    both = jnp.concatenate([high, (x - high.astype(F32)).astype(BF16)], axis=1)
    nt = (((1,), (1,)), ((), ()))
    total = lax.dot_general(jnp.ones((TAIL, 2 * width), BF16), both, nt, preferred_element_type=F32)
    inv = lax.rsqrt(total[0:1] * (1.0 / width) + EPS)
    ee = jnp.concatenate([e, e], axis=1)
    s_ref[...] = lax.dot_general(hl[pl.ds(b * size, size), :], ee, nt, preferred_element_type=F32)
    parts = []
    rows = 32
    for k in range(size // rows):
        w = jnp.exp2(s_ref[pl.ds(k * rows, rows), :] * inv - 2.0 * KERNEL_SCALE * LOG2E)
        if diagonal is not None:
            i = lax.broadcasted_iota(jnp.int32, (rows, size), 0) + k * rows
            j = lax.broadcasted_iota(jnp.int32, (rows, size), 1)
            w = jnp.where(jnp.logical_and(i == j, diagonal), 0.0, w)
        w_ref[at, pl.ds(k * rows, rows), :] = w.astype(BF16)
        parts.append(lanes_sum(w))
    return parts


def add_parts(ref, first, parts, mask, start):
    rows = parts[0].shape[0]
    for k, part in enumerate(parts):
        at = pl.ds(first + k * rows, rows)
        value = part * mask
        ref[at, :] = value if start else ref[at, :] + value


def own_weights_kernel(blocks, pack_ref, hl, w_ref, row_ref, col_ref, s_ref):
    mols = hl.shape[0]
    size, width = mols // blocks, hl.shape[1] // 2
    c = lax.axis_index("col")
    table = pack_ref[pl.ds(mols, TAIL), :].astype(F32)
    for b in range(blocks):
        x = pack_ref[pl.ds(b * size, size), :].astype(F32)
        scale = lax.rsqrt(jnp.sum(x * x, axis=-1, keepdims=True) * (1.0 / width) + EPS)
        x = x * (scale * (2.0 * KERNEL_SCALE * LOG2E / width))
        high = x.astype(BF16)
        hl[pl.ds(b * size, size), :width] = high
        hl[pl.ds(b * size, size), width:] = (x - high.astype(F32)).astype(BF16)
    e = pack_ref[pl.ds(pl.multiple_of(c * size, size), size), :]
    for b in range(blocks):
        parts = tile_weights(hl, b, e, w_ref, b, s_ref, c == b)
        from_c = jnp.where(c == 0, table_entry(table, 0, b), table_entry(table, 1, b - 1))
        add_parts(row_ref, b * size, parts, table_entry(table, b, c - b), True)
        add_parts(col_ref, b * size, parts, from_c, True)


def peer_weights_kernel(dims, offsets, pack_ref, peer_ref, hl, row_in, col_in, w_ref, *rest):
    blocks, last = dims
    if last:
        deg_ref, row_ref, col_ref, s_ref = rest
    else:
        row_ref, col_ref, s_ref = rest
    mols = hl.shape[0]
    size = mols // blocks
    chips = peer_offset(offsets)
    valid = jnp.where(chips != 0, 1.0, 0.0)
    own_table = pack_ref[pl.ds(mols, TAIL), :].astype(F32) * valid
    peer_table = peer_ref[pl.ds(mols, TAIL), :].astype(F32) * valid
    row_ref[...] = row_in[...]
    col_ref[...] = col_in[...]
    for k in range(blocks):
        e = peer_ref[pl.ds(k * size, size), :]
        for b in range(blocks):
            offset = chips * blocks + (k - b)
            parts = tile_weights(hl, b, e, w_ref, k * blocks + b, s_ref, None)
            add_parts(row_ref, b * size, parts, table_entry(own_table, b, offset), False)
            add_parts(col_ref, b * size, parts, table_entry(peer_table, k, -offset), False)
    if last:
        lane = lax.broadcasted_iota(jnp.int32, (size, LANES), 1)
        for b in range(blocks):
            at = pl.ds(b * size, size)
            by_row = jnp.sum(row_ref[at, :], axis=-1, keepdims=True)
            by_col = jnp.sum(col_ref[at, :], axis=-1, keepdims=True)
            deg_ref[at, :] = jnp.where(lane < LANES // 2, by_row, by_col)


def scale_kernel(own_ref, other_ref, seed_ref, scaled_ref, rs_ref, cs_ref):
    total = lax.rsqrt(own_ref[...] + other_ref[...])
    by_col = jnp.broadcast_to(total[:, LANES // 2 : LANES // 2 + 1], total.shape)
    rs_ref[...] = jnp.broadcast_to(total[:, 0:1] * ALPHA, total.shape)
    cs_ref[...] = by_col
    scaled_ref[...] = (seed_ref[...] * by_col).astype(BF16)


def product_kernel(blocks, offsets, pack_ref, w_ref, scaled_ref, *rest):
    out_ref = rest[-1]
    mols = scaled_ref.shape[0]
    size = mols // blocks
    table = pack_ref[pl.ds(mols, TAIL), :].astype(F32)
    c = lax.axis_index("col")
    if offsets is not None:
        chips = peer_offset(offsets)
        table = table * jnp.where(chips != 0, 1.0, 0.0)
    for b in range(blocks):
        at = pl.ds(b * size, size)
        if offsets is None:
            s = scaled_ref[pl.ds(pl.multiple_of(c * size, size), size), :].astype(F32)
            s = (s * table_entry(table, b, c - b)).astype(BF16)
            out_ref[at, :] = jnp.dot(w_ref[b], s, preferred_element_type=F32)
            continue
        total = rest[0][at, :]
        for k in range(blocks):
            offset = chips * blocks + (k - b)
            s = scaled_ref[pl.ds(k * size, size), :].astype(F32)
            s = (s * table_entry(table, b, offset)).astype(BF16)
            total = total + jnp.dot(w_ref[k * blocks + b], s, preferred_element_type=F32)
        out_ref[at, :] = total


def state_kernel(own_ref, other_ref, rs_ref, seed_ref, cs_ref, out_ref):
    state = (own_ref[...] + other_ref[...]) * rs_ref[...] + (1.0 - ALPHA) * seed_ref[...]
    out_ref[...] = (state * cs_ref[...]).astype(BF16)


def kernel_call(body, name, ins, outs, flops, scratch=(), in_specs=None):
    return pl.pallas_call(
        body,
        out_shape=outs,
        in_specs=in_specs or [VMEM] * len(ins),
        out_specs=jax.tree.map(lambda _: VMEM, outs),
        scratch_shapes=scratch,
        compiler_params=PARAMS,
        cost_estimate=pl.CostEstimate(flops=flops, bytes_accessed=1 << 20, transcendentals=0),
        name=name,
    )(*ins)


def shards(embeddings, profiles, seed_mask, tile_cols, tile_count):
    rows, cols = lax.axis_size("row"), lax.axis_size("col")
    blocks, slots = tile_cols.shape
    mols, width = embeddings.shape
    prof = profiles.shape[1]
    size = mols // blocks
    reach = (BAND + blocks - 1) // blocks
    assert blocks == 2 and cols == 2 and width == LANES and prof == LANES
    steps = swap_steps(rows, cols, reach)
    if len(steps) == 3:
        steps = [steps[1], steps[0], steps[2]]
    f32_rows = jax.ShapeDtypeStruct((mols, LANES), F32)
    bf16_rows = jax.ShapeDtypeStruct((mols, LANES), BF16)
    tile_flops = 4 * size * size * width

    def from_peers(value):
        return [lax.ppermute(value, ("row", "col"), swaps) for swaps, _ in steps]

    def other_core(value):
        return lax.ppermute(value, "col", [(0, 1), (1, 0)])

    def weights_of(tiles):
        return jax.ShapeDtypeStruct((tiles, size, size), BF16)

    held = [pltpu.with_memory_space_constraint(t, pltpu.HBM) for t in (embeddings, tile_cols, tile_count)]
    pack = kernel_call(
        lambda *refs: pack_kernel(blocks, slots, *refs),
        "pack",
        held,
        jax.ShapeDtypeStruct((mols + TAIL, LANES), BF16),
        1,
        [
            pltpu.SMEM(tile_cols.shape, jnp.int32),
            pltpu.SMEM(tile_count.shape, jnp.int32),
            pltpu.SemaphoreType.DMA((3,)),
        ],
        [HBM] * 3,
    )
    peer_packs = from_peers(pack)
    seed_rows = jnp.where(seed_mask[:, None] > 0, profiles, 0.0)
    one_tile = pltpu.VMEM((size, size), F32)
    hl, own_weights, row_sum, col_sum = kernel_call(
        lambda *refs: own_weights_kernel(blocks, *refs),
        "own_weights",
        [pack],
        (jax.ShapeDtypeStruct((mols, 2 * width), BF16), weights_of(blocks), f32_rows, f32_rows),
        blocks * tile_flops,
        [one_tile],
    )
    weights = [own_weights]
    for step, (_, offsets) in enumerate(steps):
        last = step + 1 == len(steps)
        ins = [pack, peer_packs[step], hl, row_sum, col_sum]
        out = kernel_call(
            lambda *refs, offsets=offsets, last=last: peer_weights_kernel((blocks, last), offsets, *refs),
            "peer_weights",
            ins,
            (weights_of(blocks * blocks), f32_rows) if last else (weights_of(blocks * blocks), f32_rows, f32_rows),
            blocks * blocks * tile_flops,
            [pltpu.VMEM((mols, LANES), F32)] * 2 + [one_tile] if last else [one_tile],
        )
        weights.append(out[0])
        if last:
            degree = out[1]
        else:
            row_sum, col_sum = out[1:]
    scaled, row_scale, col_scale = kernel_call(
        scale_kernel, "scale", [degree, other_core(degree), seed_rows], (bf16_rows, f32_rows, f32_rows), 1
    )
    for iteration in range(ITERS):
        peers = from_peers(scaled)
        partial = kernel_call(
            lambda *refs: product_kernel(blocks, None, *refs),
            "own_product",
            [pack, weights[0], scaled],
            f32_rows,
            blocks * tile_flops,
        )
        for step, (_, offsets) in enumerate(steps):
            partial = kernel_call(
                lambda *refs, offsets=offsets: product_kernel(blocks, offsets, *refs),
                "peer_product",
                [pack, weights[1 + step], peers[step], partial],
                f32_rows,
                blocks * blocks * tile_flops,
            )
        other = other_core(partial)
        if iteration + 1 < ITERS:
            scaled = kernel_call(
                state_kernel, "state", [partial, other, row_scale, seed_rows, col_scale], bf16_rows, 1
            )
    return (partial + other) * row_scale + (1.0 - ALPHA) * seed_rows


def solution(mesh):
    placed = (
        P(("grp", "row"), None),
        P(("grp", "row"), None),
        P(("grp", "row")),
        P(("grp", "row"), None),
        P(("grp", "row")),
    )
    return jax.shard_map(
        shards, mesh=mesh, in_specs=placed, out_specs=P(("grp", "row"), None), check_vma=False
    )
```

```python
import itertools

import jax
import jax.numpy as jnp
from jax import lax
from jax.experimental import pallas as pl
from jax.experimental.pallas import tpu as pltpu
from jax.sharding import PartitionSpec as P

BAND = 6
ITERS = 2

KERNEL_SCALE = 12.5
ALPHA = 0.8
EPS = 1e-06
LOG2E = 1.4426950408889634
LANES = 128
TAIL = 16
F32 = jnp.float32
BF16 = jnp.bfloat16

VMEM = pl.BlockSpec(memory_space=pltpu.VMEM)
HBM = pl.BlockSpec(memory_space=pltpu.HBM)
PARAMS = pltpu.CompilerParams(vmem_limit_bytes=24 * 1024 * 1024)


def search_steps(rows, reach):
    if reach != 3 or rows < 8:
        return None
    edges = [(a, a + d) for a in range(rows) for d in range(1, reach + 1) if a + d < rows]

    def solve(room):
        chosen = []

        def place(n):
            done = edges[n][0] if n < len(edges) else rows
            if any(room[chip][step] for chip in range(max(done - reach, 0), done) for step in range(reach)):
                return False
            if n == len(edges):
                return True
            a, b = edges[n]
            for k in range(reach):
                step = (b - a - 1 + k) % reach
                if room[a][step] and room[b][step]:
                    room[a][step] -= 1
                    room[b][step] -= 1
                    chosen.append(step)
                    if place(n + 1):
                        return True
                    room[a][step] += 1
                    room[b][step] += 1
                    chosen.pop()
            return False

        return chosen if place(0) else None

    best, best_moved = None, None
    orders = list(itertools.permutations(range(reach)))
    for low, near_low, high, near_high in itertools.product(orders, range(reach), orders, range(reach)):
        room = [[2] * reach for _ in range(rows)]
        for chip, way, order, near in ((0, 1, low, near_low), (rows - 1, -1, high, near_high)):
            for k in range(reach):
                room[chip][order[k]] = k
            room[chip + way][near] = 0
            room[chip + 2 * way][order[1]] = 1
        chosen = solve(room)
        if chosen is not None:
            moved = sum(step != b - a - 1 for (a, b), step in zip(edges, chosen))
            if best is None or moved < best_moved:
                best, best_moved = chosen, moved
    if best is None:
        return None
    return [[e for e, s in zip(edges, best) if s == step] for step in range(reach)]


def swap_steps(rows, cols, reach):
    chip_steps = search_steps(rows, reach)
    if chip_steps is None:
        chip_steps = [[(a, a + d) for a in range(rows - d)] for d in range(1, reach + 1)]
    steps = []
    for chip_pairs in chip_steps:
        free = [list(range(cols)) for _ in range(rows)]
        offsets = [[0] * rows for _ in range(cols)]
        swaps = []
        for a, b in chip_pairs:
            core_a, core_b = free[a].pop(0), free[b].pop(0)
            swaps.append((a * cols + core_a, b * cols + core_b))
            offsets[core_a][a], offsets[core_b][b] = b - a, a - b
        idle = []
        for chip, cores in enumerate(free):
            if len(cores) == 2:
                swaps.append((chip * cols + cores[0], chip * cols + cores[1]))
            else:
                idle += [chip * cols + core for core in cores]
        swaps += list(zip(idle[::2], idle[1::2]))
        steps.append((swaps + [(b, a) for a, b in swaps], offsets))
    return steps


def peer_offset(offsets):
    r, c = lax.axis_index("row"), lax.axis_index("col")
    value = jnp.int32(0)
    for core, per_row in enumerate(offsets):
        for word, first in enumerate(range(0, len(per_row), 8)):
            code = sum((offset + 8) << (4 * n) for n, offset in enumerate(per_row[first : first + 8]))
            code = jnp.int32(code - (1 << 32) if code >= 1 << 31 else code)
            digit = (lax.shift_right_logical(code, 4 * lax.rem(r, 8)) & 15) - 8
            here = jnp.logical_and(c == core, lax.div(r, 8) == word)
            value = jnp.where(here, digit, value)
    return value


def table_entry(table, row, offset):
    lane = lax.broadcasted_iota(jnp.int32, (1, LANES), 1)
    return jnp.max(jnp.where(lane == offset + BAND, table[row : row + 1, :], 0.0), axis=-1, keepdims=True)


def lanes_sum(w):
    part = w[:, :LANES]
    for k in range(1, w.shape[1] // LANES):
        part = part + w[:, k * LANES : (k + 1) * LANES]
    return part


def listing_table(blocks, slots, cols_ref, count_ref):
    first = lax.axis_index("row") * blocks
    lane = lax.broadcasted_iota(jnp.int32, (8, LANES), 1)
    row = lax.broadcasted_iota(jnp.int32, (8, LANES), 0)
    table = jnp.zeros((8, LANES), F32)
    for b in range(blocks):
        for s in range(slots):
            offset = jnp.where(s < count_ref[b], cols_ref[b, s] - (first + b) + BAND, -1)
            table = jnp.where(jnp.logical_and(lane == offset, row == b), 1.0, table)
    return table


def compact(column):
    eye = lax.broadcasted_iota(jnp.int32, (LANES, LANES), 0) == lax.broadcasted_iota(jnp.int32, (LANES, LANES), 1)
    rows = []
    for k in range(column.shape[0] // LANES):
        rows.append(jnp.sum(jnp.where(eye, column[k * LANES : (k + 1) * LANES], 0.0), axis=0, keepdims=True))
    return jnp.concatenate(rows, axis=0)


def tile_weights(hl, b, e, w_ref, at, s_ref, diagonal):
    size, width = e.shape
    x = e.astype(F32)
    x = x * x
    high = x.astype(BF16)
    both = jnp.concatenate([high, (x - high.astype(F32)).astype(BF16)], axis=1)
    nt = (((1,), (1,)), ((), ()))
    total = lax.dot_general(jnp.ones((TAIL, 2 * width), BF16), both, nt, preferred_element_type=F32)
    inv = lax.rsqrt(total[0:1] * (1.0 / width) + EPS)
    ee = jnp.concatenate([e, e], axis=1)
    s_ref[...] = lax.dot_general(hl[pl.ds(b * size, size), :], ee, nt, preferred_element_type=F32)
    parts = []
    rows = 32
    for k in range(size // rows):
        w = jnp.exp2(s_ref[pl.ds(k * rows, rows), :] * inv - 2.0 * KERNEL_SCALE * LOG2E)
        if diagonal is not None:
            i = lax.broadcasted_iota(jnp.int32, (rows, size), 0) + k * rows
            j = lax.broadcasted_iota(jnp.int32, (rows, size), 1)
            w = jnp.where(jnp.logical_and(i == j, diagonal), 0.0, w)
        w_ref[at, pl.ds(k * rows, rows), :] = w.astype(BF16)
        parts.append(lanes_sum(w))
    return parts


def add_parts(ref, first, parts, mask, start):
    rows = parts[0].shape[0]
    for k, part in enumerate(parts):
        at = pl.ds(first + k * rows, rows)
        value = part * mask
        ref[at, :] = value if start else ref[at, :] + value


def own_weights_kernel(dims, cols_hbm, count_hbm, own_hbm, *rest):
    blocks, slots = dims
    table_ref, hl, w_ref, row_ref, col_ref, s_ref, own_ref, cols_ref, count_ref, sems = rest
    loads = [
        pltpu.make_async_copy(cols_hbm, cols_ref, sems.at[0]),
        pltpu.make_async_copy(count_hbm, count_ref, sems.at[1]),
        pltpu.make_async_copy(own_hbm, own_ref, sems.at[2]),
    ]
    for load in loads:
        load.start()
    for load in loads:
        load.wait()
    mols = hl.shape[0]
    size, width = mols // blocks, hl.shape[1] // 2
    c = lax.axis_index("col")
    table = listing_table(blocks, slots, cols_ref, count_ref)
    table_ref[...] = table
    for b in range(blocks):
        x = own_ref[pl.ds(b * size, size), :].astype(F32)
        scale = lax.rsqrt(jnp.sum(x * x, axis=-1, keepdims=True) * (1.0 / width) + EPS)
        x = x * (scale * (2.0 * KERNEL_SCALE * LOG2E / width))
        high = x.astype(BF16)
        hl[pl.ds(b * size, size), :width] = high
        hl[pl.ds(b * size, size), width:] = (x - high.astype(F32)).astype(BF16)
    e = own_ref[pl.ds(pl.multiple_of(c * size, size), size), :]
    for b in range(blocks):
        parts = tile_weights(hl, b, e, w_ref, b, s_ref, c == b)
        from_c = jnp.where(c == 0, table_entry(table, 0, b), table_entry(table, 1, b - 1))
        add_parts(row_ref, b * size, parts, table_entry(table, b, c - b), True)
        add_parts(col_ref, b * size, parts, from_c, True)


def peer_weights_kernel(dims, offsets, table_ref, peer_ref, peer_table_ref, hl, row_in, col_in, w_ref, *rest):
    blocks, last = dims
    if last:
        deg_ref, row_ref, col_ref, s_ref = rest
    else:
        row_ref, col_ref, s_ref = rest
    mols = hl.shape[0]
    size = mols // blocks
    chips = peer_offset(offsets)
    valid = jnp.where(chips != 0, 1.0, 0.0)
    own_table = table_ref[...] * valid
    peer_table = peer_table_ref[...] * valid
    row_ref[...] = row_in[...]
    col_ref[...] = col_in[...]
    for k in range(blocks):
        e = peer_ref[pl.ds(k * size, size), :]
        for b in range(blocks):
            offset = chips * blocks + (k - b)
            parts = tile_weights(hl, b, e, w_ref, k * blocks + b, s_ref, None)
            add_parts(row_ref, b * size, parts, table_entry(own_table, b, offset), False)
            add_parts(col_ref, b * size, parts, table_entry(peer_table, k, -offset), False)
    if last:
        half = mols // LANES
        for n, ref in enumerate((row_ref, col_ref)):
            deg_ref[pl.ds(n * half, half), :] = compact(jnp.sum(ref[...], axis=-1, keepdims=True))


def seeds_kernel(mask_ref, profile_ref, after_ref, seed_ref, bf16_ref):
    del after_ref
    columns = mask_ref[...].astype(F32).T
    for k in range(mask_ref.shape[0]):
        at = pl.ds(k * LANES, LANES)
        seed = jnp.where(columns[:, k : k + 1] > 0.0, profile_ref[at, :], 0.0)
        seed_ref[at, :] = seed
        bf16_ref[at, :] = seed.astype(BF16)


def degree_kernel(own_ref, other_ref, out_ref):
    out_ref[...] = lax.rsqrt(own_ref[...] + other_ref[...])


def expand_kernel(scales_ref, seed_ref, scaled_ref, rs_ref, cs_ref):
    columns = scales_ref[...].T
    half = scales_ref.shape[0] // 2
    for k in range(half):
        at = pl.ds(k * LANES, LANES)
        by_col = jnp.broadcast_to(columns[:, half + k : half + k + 1], (LANES, LANES))
        rs_ref[at, :] = jnp.broadcast_to(columns[:, k : k + 1] * ALPHA, (LANES, LANES))
        cs_ref[at, :] = by_col
        scaled_ref[at, :] = (seed_ref[at, :] * by_col).astype(BF16)


def product_kernel(blocks, offsets, first, table_ref, w_ref, scaled_ref, *rest):
    if first:
        scales_ref, _, out_ref, product_ref = rest
        columns = scales_ref[...].T
        half = scales_ref.shape[0] // 2
        for k in range(half):
            at = pl.ds(k * LANES, LANES)
            seed = scaled_ref[at, :].astype(F32)
            product_ref[at, :] = (seed * columns[:, half + k : half + k + 1]).astype(BF16)
        scaled_ref, rest = product_ref, rest[1:]
    else:
        out_ref = rest[-1]
    mols = scaled_ref.shape[0]
    size = mols // blocks
    table = table_ref[...]
    c = lax.axis_index("col")
    if offsets is not None:
        chips = peer_offset(offsets)
        table = table * jnp.where(chips != 0, 1.0, 0.0)
    for b in range(blocks):
        at = pl.ds(b * size, size)
        if offsets is None:
            s = scaled_ref[pl.ds(pl.multiple_of(c * size, size), size), :].astype(F32)
            s = (s * table_entry(table, b, c - b)).astype(BF16)
            out_ref[at, :] = jnp.dot(w_ref[b], s, preferred_element_type=F32)
            continue
        total = rest[0][at, :]
        for k in range(blocks):
            offset = chips * blocks + (k - b)
            s = scaled_ref[pl.ds(k * size, size), :].astype(F32)
            s = (s * table_entry(table, b, offset)).astype(BF16)
            total = total + jnp.dot(w_ref[k * blocks + b], s, preferred_element_type=F32)
        out_ref[at, :] = total


def state_kernel(own_ref, other_ref, rs_ref, seed_ref, cs_ref, out_ref):
    state = (own_ref[...] + other_ref[...]) * rs_ref[...] + (1.0 - ALPHA) * seed_ref[...]
    out_ref[...] = (state * cs_ref[...]).astype(BF16)


def kernel_call(body, name, ins, outs, flops, scratch=(), in_specs=None):
    return pl.pallas_call(
        body,
        out_shape=outs,
        in_specs=in_specs or [VMEM] * len(ins),
        out_specs=jax.tree.map(lambda _: VMEM, outs),
        scratch_shapes=scratch,
        compiler_params=PARAMS,
        cost_estimate=pl.CostEstimate(flops=flops, bytes_accessed=1 << 20, transcendentals=0),
        name=name,
    )(*ins)


def shards(embeddings, profiles, seed_mask, tile_cols, tile_count):
    rows, cols = lax.axis_size("row"), lax.axis_size("col")
    blocks, slots = tile_cols.shape
    mols, width = embeddings.shape
    prof = profiles.shape[1]
    size = mols // blocks
    reach = (BAND + blocks - 1) // blocks
    assert blocks == 2 and cols == 2 and width == LANES and prof == LANES
    steps = swap_steps(rows, cols, reach)
    if len(steps) == 3:
        steps = [steps[1], steps[0], steps[2]]
    f32_rows = jax.ShapeDtypeStruct((mols, LANES), F32)
    bf16_rows = jax.ShapeDtypeStruct((mols, LANES), BF16)
    tile_flops = 4 * size * size * width

    def to_peer(value, step):
        return lax.ppermute(value, ("row", "col"), steps[step][0])

    def from_peers(value):
        return [to_peer(value, step) for step in range(len(steps))]

    def other_core(value):
        return lax.ppermute(value, "col", [(0, 1), (1, 0)])

    def weights_of(tiles):
        return jax.ShapeDtypeStruct((tiles, size, size), BF16)

    chunks = mols // LANES
    peer_emb = from_peers(embeddings)
    one_tile = pltpu.VMEM((size, size), F32)
    table, hl, own_weights, row_sum, col_sum = kernel_call(
        lambda *refs: own_weights_kernel((blocks, slots), *refs),
        "own_weights",
        [pltpu.with_memory_space_constraint(t, pltpu.HBM) for t in (tile_cols, tile_count, embeddings)],
        (
            jax.ShapeDtypeStruct((8, LANES), F32),
            jax.ShapeDtypeStruct((mols, 2 * width), BF16),
            weights_of(blocks),
            f32_rows,
            f32_rows,
        ),
        blocks * tile_flops,
        [
            one_tile,
            pltpu.VMEM((mols, width), BF16),
            pltpu.SMEM(tile_cols.shape, jnp.int32),
            pltpu.SMEM(tile_count.shape, jnp.int32),
            pltpu.SemaphoreType.DMA((3,)),
        ],
        [HBM] * 3,
    )
    sent_table = table
    weights = [own_weights]
    for step, (_, offsets) in enumerate(steps):
        last = step + 1 == len(steps)
        if last:
            seed_rows, seeds = kernel_call(
                seeds_kernel, "seeds", [seed_mask.reshape(chunks, LANES), profiles, row_sum], (f32_rows, bf16_rows), 1
            )
            peer_seeds = from_peers(seeds)
        peer_table = to_peer(sent_table, step)
        ins = [table, peer_emb[step], peer_table, hl, row_sum, col_sum]
        degrees = jax.ShapeDtypeStruct((2 * chunks, LANES), F32)
        out = kernel_call(
            lambda *refs, offsets=offsets, last=last: peer_weights_kernel((blocks, last), offsets, *refs),
            "peer_weights",
            ins,
            (weights_of(blocks * blocks), degrees) if last else (weights_of(blocks * blocks), f32_rows, f32_rows),
            blocks * blocks * tile_flops,
            [pltpu.VMEM((mols, LANES), F32)] * 2 + [one_tile] if last else [one_tile],
        )
        weights.append(out[0])
        if last:
            degree = out[1]
        else:
            row_sum, col_sum = out[1:]
            if step + 3 == len(steps):
                sent_table, row_sum = lax.optimization_barrier((table, row_sum))
    scales = kernel_call(degree_kernel, "degree", [degree, other_core(degree)], degrees, 1)
    scales, peer_seeds[0] = lax.optimization_barrier((scales, peer_seeds[0]))
    peer_scales = from_peers(scales)
    scaled, row_scale, col_scale = kernel_call(
        expand_kernel, "expand", [scales, seed_rows], (bf16_rows, f32_rows, f32_rows), 1
    )
    for iteration in range(ITERS):
        first = iteration == 0
        peers = peer_seeds if first else from_peers(scaled)
        partial = kernel_call(
            lambda *refs: product_kernel(blocks, None, False, *refs),
            "own_product",
            [table, weights[0], scaled],
            f32_rows,
            blocks * tile_flops,
        )
        for step, (_, offsets) in enumerate(steps):
            partial = kernel_call(
                lambda *refs, offsets=offsets, first=first: product_kernel(blocks, offsets, first, *refs),
                "peer_product",
                [table, weights[1 + step], peers[step]] + [peer_scales[step]] * first + [partial],
                f32_rows,
                blocks * blocks * tile_flops,
                [pltpu.VMEM((mols, LANES), BF16)] * first,
            )
        other = other_core(partial)
        if iteration + 1 < ITERS:
            scaled = kernel_call(
                state_kernel, "state", [partial, other, row_scale, seed_rows, col_scale], bf16_rows, 1
            )
    return (partial + other) * row_scale + (1.0 - ALPHA) * seed_rows


def solution(mesh):
    placed = (
        P(("grp", "row"), None),
        P(("grp", "row"), None),
        P(("grp", "row")),
        P(("grp", "row"), None),
        P(("grp", "row")),
    )
    return jax.shard_map(
        shards, mesh=mesh, in_specs=placed, out_specs=P(("grp", "row"), None), check_vma=False
    )
```

```python
import itertools

import jax
import jax.numpy as jnp
from jax import lax
from jax.experimental import pallas as pl
from jax.experimental.pallas import tpu as pltpu
from jax.sharding import PartitionSpec as P

BAND = 6
ITERS = 2

KERNEL_SCALE = 12.5
ALPHA = 0.8
EPS = 1e-06
LOG2E = 1.4426950408889634
LANES = 128
TAIL = 16
F32 = jnp.float32
BF16 = jnp.bfloat16

VMEM = pl.BlockSpec(memory_space=pltpu.VMEM)
HBM = pl.BlockSpec(memory_space=pltpu.HBM)
PARAMS = pltpu.CompilerParams(vmem_limit_bytes=24 * 1024 * 1024)


def search_steps(rows, reach):
    if reach != 3 or rows < 8:
        return None
    edges = [(a, a + d) for a in range(rows) for d in range(1, reach + 1) if a + d < rows]

    def solve(room):
        chosen = []

        def place(n):
            done = edges[n][0] if n < len(edges) else rows
            if any(room[chip][step] for chip in range(max(done - reach, 0), done) for step in range(reach)):
                return False
            if n == len(edges):
                return True
            a, b = edges[n]
            for k in range(reach):
                step = (b - a - 1 + k) % reach
                if room[a][step] and room[b][step]:
                    room[a][step] -= 1
                    room[b][step] -= 1
                    chosen.append(step)
                    if place(n + 1):
                        return True
                    room[a][step] += 1
                    room[b][step] += 1
                    chosen.pop()
            return False

        return chosen if place(0) else None

    best, best_moved = None, None
    orders = list(itertools.permutations(range(reach)))
    for low, near_low, high, near_high in itertools.product(orders, range(reach), orders, range(reach)):
        room = [[2] * reach for _ in range(rows)]
        for chip, way, order, near in ((0, 1, low, near_low), (rows - 1, -1, high, near_high)):
            for k in range(reach):
                room[chip][order[k]] = k
            room[chip + way][near] = 0
            room[chip + 2 * way][order[1]] = 1
        chosen = solve(room)
        if chosen is not None:
            moved = sum(step != b - a - 1 for (a, b), step in zip(edges, chosen))
            if best is None or moved < best_moved:
                best, best_moved = chosen, moved
    if best is None:
        return None
    return [[e for e, s in zip(edges, best) if s == step] for step in range(reach)]


def swap_steps(rows, cols, reach):
    chip_steps = search_steps(rows, reach)
    if chip_steps is None:
        chip_steps = [[(a, a + d) for a in range(rows - d)] for d in range(1, reach + 1)]
    steps = []
    for chip_pairs in chip_steps:
        free = [list(range(cols)) for _ in range(rows)]
        offsets = [[0] * rows for _ in range(cols)]
        swaps = []
        for a, b in chip_pairs:
            core_a, core_b = free[a].pop(0), free[b].pop(0)
            swaps.append((a * cols + core_a, b * cols + core_b))
            offsets[core_a][a], offsets[core_b][b] = b - a, a - b
        idle = []
        for chip, cores in enumerate(free):
            if len(cores) == 2:
                swaps.append((chip * cols + cores[0], chip * cols + cores[1]))
            else:
                idle += [chip * cols + core for core in cores]
        swaps += list(zip(idle[::2], idle[1::2]))
        steps.append((swaps + [(b, a) for a, b in swaps], offsets))
    return steps


def peer_offset(offsets):
    r, c = lax.axis_index("row"), lax.axis_index("col")
    value = jnp.int32(0)
    for core, per_row in enumerate(offsets):
        for word, first in enumerate(range(0, len(per_row), 8)):
            code = sum((offset + 8) << (4 * n) for n, offset in enumerate(per_row[first : first + 8]))
            code = jnp.int32(code - (1 << 32) if code >= 1 << 31 else code)
            digit = (lax.shift_right_logical(code, 4 * lax.rem(r, 8)) & 15) - 8
            here = jnp.logical_and(c == core, lax.div(r, 8) == word)
            value = jnp.where(here, digit, value)
    return value


def table_entry(table, row, offset):
    lane = lax.broadcasted_iota(jnp.int32, (1, LANES), 1)
    return jnp.max(jnp.where(lane == offset + BAND, table[row : row + 1, :], 0.0), axis=-1, keepdims=True)


def lanes_sum(w):
    part = w[:, :LANES]
    for k in range(1, w.shape[1] // LANES):
        part = part + w[:, k * LANES : (k + 1) * LANES]
    return part


def pack_kernel(blocks, slots, emb_hbm, cols_hbm, count_hbm, out_ref, cols_ref, count_ref, sems):
    mols = emb_hbm.shape[0]
    loads = [
        pltpu.make_async_copy(emb_hbm, out_ref.at[pl.ds(0, mols), :], sems.at[0]),
        pltpu.make_async_copy(cols_hbm, cols_ref, sems.at[1]),
        pltpu.make_async_copy(count_hbm, count_ref, sems.at[2]),
    ]
    for load in loads:
        load.start()
    loads[1].wait()
    loads[2].wait()
    first = lax.axis_index("row") * blocks
    lane = lax.broadcasted_iota(jnp.int32, (TAIL, LANES), 1)
    row = lax.broadcasted_iota(jnp.int32, (TAIL, LANES), 0)
    table = jnp.zeros((TAIL, LANES), F32)
    for b in range(blocks):
        for s in range(slots):
            offset = jnp.where(s < count_ref[b], cols_ref[b, s] - (first + b) + BAND, -1)
            table = jnp.where(jnp.logical_and(lane == offset, row == b), 1.0, table)
    out_ref[pl.ds(mols, TAIL), :] = table.astype(BF16)
    loads[0].wait()


def compact(column):
    eye = lax.broadcasted_iota(jnp.int32, (LANES, LANES), 0) == lax.broadcasted_iota(jnp.int32, (LANES, LANES), 1)
    rows = []
    for k in range(column.shape[0] // LANES):
        rows.append(jnp.sum(jnp.where(eye, column[k * LANES : (k + 1) * LANES], 0.0), axis=0, keepdims=True))
    return jnp.concatenate(rows, axis=0)


def tile_weights(hl, b, e, w_ref, at, s_ref, diagonal):
    size, width = e.shape
    x = e.astype(F32)
    x = x * x
    high = x.astype(BF16)
    both = jnp.concatenate([high, (x - high.astype(F32)).astype(BF16)], axis=1)
    nt = (((1,), (1,)), ((), ()))
    total = lax.dot_general(jnp.ones((TAIL, 2 * width), BF16), both, nt, preferred_element_type=F32)
    inv = lax.rsqrt(total[0:1] * (1.0 / width) + EPS)
    ee = jnp.concatenate([e, e], axis=1)
    s_ref[...] = lax.dot_general(hl[pl.ds(b * size, size), :], ee, nt, preferred_element_type=F32)
    parts = []
    rows = 32
    for k in range(size // rows):
        w = jnp.exp2(s_ref[pl.ds(k * rows, rows), :] * inv - 2.0 * KERNEL_SCALE * LOG2E)
        if diagonal is not None:
            i = lax.broadcasted_iota(jnp.int32, (rows, size), 0) + k * rows
            j = lax.broadcasted_iota(jnp.int32, (rows, size), 1)
            w = jnp.where(jnp.logical_and(i == j, diagonal), 0.0, w)
        w_ref[at, pl.ds(k * rows, rows), :] = w.astype(BF16)
        parts.append(lanes_sum(w))
    return parts


def add_parts(ref, first, parts, mask, start):
    rows = parts[0].shape[0]
    for k, part in enumerate(parts):
        at = pl.ds(first + k * rows, rows)
        value = part * mask
        ref[at, :] = value if start else ref[at, :] + value


def own_weights_kernel(blocks, pack_ref, hl, w_ref, row_ref, col_ref, s_ref):
    mols = hl.shape[0]
    size, width = mols // blocks, hl.shape[1] // 2
    c = lax.axis_index("col")
    table = pack_ref[pl.ds(mols, TAIL), :].astype(F32)
    for b in range(blocks):
        x = pack_ref[pl.ds(b * size, size), :].astype(F32)
        scale = lax.rsqrt(jnp.sum(x * x, axis=-1, keepdims=True) * (1.0 / width) + EPS)
        x = x * (scale * (2.0 * KERNEL_SCALE * LOG2E / width))
        high = x.astype(BF16)
        hl[pl.ds(b * size, size), :width] = high
        hl[pl.ds(b * size, size), width:] = (x - high.astype(F32)).astype(BF16)
    e = pack_ref[pl.ds(pl.multiple_of(c * size, size), size), :]
    for b in range(blocks):
        parts = tile_weights(hl, b, e, w_ref, b, s_ref, c == b)
        from_c = jnp.where(c == 0, table_entry(table, 0, b), table_entry(table, 1, b - 1))
        add_parts(row_ref, b * size, parts, table_entry(table, b, c - b), True)
        add_parts(col_ref, b * size, parts, from_c, True)


def peer_weights_kernel(dims, offsets, pack_ref, peer_ref, hl, row_in, col_in, w_ref, *rest):
    blocks, last = dims
    if last:
        deg_ref, row_ref, col_ref, s_ref = rest
    else:
        row_ref, col_ref, s_ref = rest
    mols = hl.shape[0]
    size = mols // blocks
    chips = peer_offset(offsets)
    valid = jnp.where(chips != 0, 1.0, 0.0)
    own_table = pack_ref[pl.ds(mols, TAIL), :].astype(F32) * valid
    peer_table = peer_ref[pl.ds(mols, TAIL), :].astype(F32) * valid
    row_ref[...] = row_in[...]
    col_ref[...] = col_in[...]
    for k in range(blocks):
        e = peer_ref[pl.ds(k * size, size), :]
        for b in range(blocks):
            offset = chips * blocks + (k - b)
            parts = tile_weights(hl, b, e, w_ref, k * blocks + b, s_ref, None)
            add_parts(row_ref, b * size, parts, table_entry(own_table, b, offset), False)
            add_parts(col_ref, b * size, parts, table_entry(peer_table, k, -offset), False)
    if last:
        half = mols // LANES
        for n, ref in enumerate((row_ref, col_ref)):
            deg_ref[pl.ds(n * half, half), :] = compact(jnp.sum(ref[...], axis=-1, keepdims=True))


def seeds_kernel(mask_ref, profile_ref, after_ref, seed_ref, bf16_ref):
    del after_ref
    columns = mask_ref[...].astype(F32).T
    for k in range(mask_ref.shape[0]):
        at = pl.ds(k * LANES, LANES)
        seed = jnp.where(columns[:, k : k + 1] > 0.0, profile_ref[at, :], 0.0)
        seed_ref[at, :] = seed
        bf16_ref[at, :] = seed.astype(BF16)


def degree_kernel(own_ref, other_ref, out_ref):
    out_ref[...] = lax.rsqrt(own_ref[...] + other_ref[...])


def expand_kernel(scales_ref, seed_ref, scaled_ref, rs_ref, cs_ref):
    columns = scales_ref[...].T
    half = scales_ref.shape[0] // 2
    for k in range(half):
        at = pl.ds(k * LANES, LANES)
        by_col = jnp.broadcast_to(columns[:, half + k : half + k + 1], (LANES, LANES))
        rs_ref[at, :] = jnp.broadcast_to(columns[:, k : k + 1] * ALPHA, (LANES, LANES))
        cs_ref[at, :] = by_col
        scaled_ref[at, :] = (seed_ref[at, :] * by_col).astype(BF16)


def product_kernel(blocks, offsets, first, pack_ref, w_ref, scaled_ref, *rest):
    if first:
        scales_ref, _, out_ref, product_ref = rest
        columns = scales_ref[...].T
        half = scales_ref.shape[0] // 2
        for k in range(half):
            at = pl.ds(k * LANES, LANES)
            seed = scaled_ref[at, :].astype(F32)
            product_ref[at, :] = (seed * columns[:, half + k : half + k + 1]).astype(BF16)
        scaled_ref, rest = product_ref, rest[1:]
    else:
        out_ref = rest[-1]
    mols = scaled_ref.shape[0]
    size = mols // blocks
    table = pack_ref[pl.ds(mols, TAIL), :].astype(F32)
    c = lax.axis_index("col")
    if offsets is not None:
        chips = peer_offset(offsets)
        table = table * jnp.where(chips != 0, 1.0, 0.0)
    for b in range(blocks):
        at = pl.ds(b * size, size)
        if offsets is None:
            s = scaled_ref[pl.ds(pl.multiple_of(c * size, size), size), :].astype(F32)
            s = (s * table_entry(table, b, c - b)).astype(BF16)
            out_ref[at, :] = jnp.dot(w_ref[b], s, preferred_element_type=F32)
            continue
        total = rest[0][at, :]
        for k in range(blocks):
            offset = chips * blocks + (k - b)
            s = scaled_ref[pl.ds(k * size, size), :].astype(F32)
            s = (s * table_entry(table, b, offset)).astype(BF16)
            total = total + jnp.dot(w_ref[k * blocks + b], s, preferred_element_type=F32)
        out_ref[at, :] = total


def state_kernel(own_ref, other_ref, rs_ref, seed_ref, cs_ref, out_ref):
    state = (own_ref[...] + other_ref[...]) * rs_ref[...] + (1.0 - ALPHA) * seed_ref[...]
    out_ref[...] = (state * cs_ref[...]).astype(BF16)


def kernel_call(body, name, ins, outs, flops, scratch=(), in_specs=None):
    return pl.pallas_call(
        body,
        out_shape=outs,
        in_specs=in_specs or [VMEM] * len(ins),
        out_specs=jax.tree.map(lambda _: VMEM, outs),
        scratch_shapes=scratch,
        compiler_params=PARAMS,
        cost_estimate=pl.CostEstimate(flops=flops, bytes_accessed=1 << 20, transcendentals=0),
        name=name,
    )(*ins)


def shards(embeddings, profiles, seed_mask, tile_cols, tile_count):
    rows, cols = lax.axis_size("row"), lax.axis_size("col")
    blocks, slots = tile_cols.shape
    mols, width = embeddings.shape
    prof = profiles.shape[1]
    size = mols // blocks
    reach = (BAND + blocks - 1) // blocks
    assert blocks == 2 and cols == 2 and width == LANES and prof == LANES
    steps = swap_steps(rows, cols, reach)
    if len(steps) == 3:
        steps = [steps[1], steps[0], steps[2]]
    f32_rows = jax.ShapeDtypeStruct((mols, LANES), F32)
    bf16_rows = jax.ShapeDtypeStruct((mols, LANES), BF16)
    tile_flops = 4 * size * size * width

    def to_peer(value, step):
        return lax.ppermute(value, ("row", "col"), steps[step][0])

    def from_peers(value):
        return [to_peer(value, step) for step in range(len(steps))]

    def other_core(value):
        return lax.ppermute(value, "col", [(0, 1), (1, 0)])

    def weights_of(tiles):
        return jax.ShapeDtypeStruct((tiles, size, size), BF16)

    chunks = mols // LANES
    held = [pltpu.with_memory_space_constraint(t, pltpu.HBM) for t in (embeddings, tile_cols, tile_count)]
    pack = kernel_call(
        lambda *refs: pack_kernel(blocks, slots, *refs),
        "pack",
        held,
        jax.ShapeDtypeStruct((mols + TAIL, LANES), BF16),
        1,
        [
            pltpu.SMEM(tile_cols.shape, jnp.int32),
            pltpu.SMEM(tile_count.shape, jnp.int32),
            pltpu.SemaphoreType.DMA((3,)),
        ],
        [HBM] * 3,
    )
    peer_packs = from_peers(pack)
    one_tile = pltpu.VMEM((size, size), F32)
    hl, own_weights, row_sum, col_sum = kernel_call(
        lambda *refs: own_weights_kernel(blocks, *refs),
        "own_weights",
        [pack],
        (jax.ShapeDtypeStruct((mols, 2 * width), BF16), weights_of(blocks), f32_rows, f32_rows),
        blocks * tile_flops,
        [one_tile],
    )
    weights = [own_weights]
    for step, (_, offsets) in enumerate(steps):
        last = step + 1 == len(steps)
        if last:
            seed_rows, seeds = kernel_call(
                seeds_kernel, "seeds", [seed_mask.reshape(chunks, LANES), profiles, row_sum], (f32_rows, bf16_rows), 1
            )
            peer_seeds = from_peers(seeds)
        ins = [pack, peer_packs[step], hl, row_sum, col_sum]
        degrees = jax.ShapeDtypeStruct((2 * chunks, LANES), F32)
        out = kernel_call(
            lambda *refs, offsets=offsets, last=last: peer_weights_kernel((blocks, last), offsets, *refs),
            "peer_weights",
            ins,
            (weights_of(blocks * blocks), degrees) if last else (weights_of(blocks * blocks), f32_rows, f32_rows),
            blocks * blocks * tile_flops,
            [pltpu.VMEM((mols, LANES), F32)] * 2 + [one_tile] if last else [one_tile],
        )
        weights.append(out[0])
        if last:
            degree = out[1]
        else:
            row_sum, col_sum = out[1:]
    scales = kernel_call(degree_kernel, "degree", [degree, other_core(degree)], degrees, 1)
    scales, peer_seeds[0] = lax.optimization_barrier((scales, peer_seeds[0]))
    peer_scales = from_peers(scales)
    scaled, row_scale, col_scale = kernel_call(
        expand_kernel, "expand", [scales, seed_rows], (bf16_rows, f32_rows, f32_rows), 1
    )
    for iteration in range(ITERS):
        first = iteration == 0
        peers = peer_seeds if first else from_peers(scaled)
        partial = kernel_call(
            lambda *refs: product_kernel(blocks, None, False, *refs),
            "own_product",
            [pack, weights[0], scaled],
            f32_rows,
            blocks * tile_flops,
        )
        for step, (_, offsets) in enumerate(steps):
            partial = kernel_call(
                lambda *refs, offsets=offsets, first=first: product_kernel(blocks, offsets, first, *refs),
                "peer_product",
                [pack, weights[1 + step], peers[step]] + [peer_scales[step]] * first + [partial],
                f32_rows,
                blocks * blocks * tile_flops,
                [pltpu.VMEM((mols, LANES), BF16)] * first,
            )
        other = other_core(partial)
        if iteration + 1 < ITERS:
            scaled = kernel_call(
                state_kernel, "state", [partial, other, row_scale, seed_rows, col_scale], bf16_rows, 1
            )
    return (partial + other) * row_scale + (1.0 - ALPHA) * seed_rows


def solution(mesh):
    placed = (
        P(("grp", "row"), None),
        P(("grp", "row"), None),
        P(("grp", "row")),
        P(("grp", "row"), None),
        P(("grp", "row")),
    )
    return jax.shard_map(
        shards, mesh=mesh, in_specs=placed, out_specs=P(("grp", "row"), None), check_vma=False
    )
```

```python
import jax
import jax.numpy as jnp
from jax import lax
from jax.experimental import pallas as pl
from jax.experimental.pallas import tpu as pltpu
from jax.sharding import PartitionSpec as P

BAND = 6
ITERS = 2

KERNEL_SCALE = 12.5
ALPHA = 0.8
EPS = 1e-06
LOG2E = 1.4426950408889634
LANES = 128
TAIL = 16
F32 = jnp.float32
BF16 = jnp.bfloat16

VMEM = pl.BlockSpec(memory_space=pltpu.VMEM)
HBM = pl.BlockSpec(memory_space=pltpu.HBM)
PARAMS = pltpu.CompilerParams(vmem_limit_bytes=24 * 1024 * 1024)


FORWARD = (True, True, True)


def distance_of(chip, device, cols):
    return abs(chip - device // cols)


def complete(moves, rows, cols, fixed):
    moves = dict(moves)
    sources = [n for n in range(rows * cols) if n not in moves]
    targets = [n for n in range(rows * cols) if n not in moves.values()]
    for s in list(sources):
        other = [t for t in targets if t // cols == s // cols and t != s]
        if other:
            moves[s] = other[0]
            sources.remove(s)
            targets.remove(other[0])
    for s in list(sources):
        if s in targets:
            y = s ^ 1
            if fixed:
                moves[s] = moves[y]
                moves[y] = s
            else:
                z = next(n for n, t in moves.items() if t == y)
                moves[z] = s
                moves[s] = y
            sources.remove(s)
            targets.remove(s)
    for s, t in zip(sources, targets):
        moves[s] = t
    return moves


def landings(moves, origin, rows, cols, distance):
    table = [[0] * rows for _ in range(cols)]
    for s, t in moves.items():
        if origin(s) is not None and distance_of(origin(s), t, cols) == distance:
            table[t % cols][t // cols] = origin(s) - t // cols
    return table


def exchange_steps(rows, cols, reach):
    steps = []
    for d in range(1, reach + 1):
        if d < 3:
            moves = {}
            for a in range(rows - d):
                core = a // d % cols
                moves[a * cols + core] = (a + d) * cols + core
                moves[(a + d) * cols + core] = a * cols + core
            moves = complete(moves, rows, cols, False)
            table = landings(moves, lambda s: s // cols, rows, cols, d)
            steps.append((moves, table, moves))
            continue
        held = steps[d - 3][1]

        def origin(s, held=held):
            offset = held[s % cols][s // cols]
            return s // cols + offset if offset else None

        moves, taken = {}, [0] * rows
        for s in range(rows * cols):
            if origin(s) is not None:
                t = s // cols + (2 if origin(s) < s // cols else -2)
                if 0 <= t < rows:
                    moves[s] = t * cols + taken[t]
                    taken[t] += 1
        moves = complete(moves, rows, cols, False)
        table = landings(moves, origin, rows, cols, d)
        direct, sent = {}, [0] * rows
        for chip in range(rows):
            for core in range(cols):
                if table[core][chip]:
                    source = chip + table[core][chip]
                    direct[source * cols + sent[source]] = chip * cols + core
                    sent[source] += 1
        direct = complete(direct, rows, cols, True)
        steps.append((moves, table, direct))
    return steps


def peer_offset(offsets):
    r, c = lax.axis_index("row"), lax.axis_index("col")
    value = jnp.int32(0)
    for core, per_row in enumerate(offsets):
        for word, first in enumerate(range(0, len(per_row), 8)):
            code = sum((offset + 8) << (4 * n) for n, offset in enumerate(per_row[first : first + 8]))
            code = jnp.int32(code - (1 << 32) if code >= 1 << 31 else code)
            digit = (lax.shift_right_logical(code, 4 * lax.rem(r, 8)) & 15) - 8
            here = jnp.logical_and(c == core, lax.div(r, 8) == word)
            value = jnp.where(here, digit, value)
    return value


def table_entry(table, row, offset):
    lane = lax.broadcasted_iota(jnp.int32, (1, LANES), 1)
    return jnp.max(jnp.where(lane == offset + BAND, table[row : row + 1, :], 0.0), axis=-1, keepdims=True)


def lanes_sum(w):
    part = w[:, :LANES]
    for k in range(1, w.shape[1] // LANES):
        part = part + w[:, k * LANES : (k + 1) * LANES]
    return part


def pack_kernel(blocks, slots, emb_hbm, cols_hbm, count_hbm, out_ref, cols_ref, count_ref, sems):
    mols = emb_hbm.shape[0]
    loads = [
        pltpu.make_async_copy(emb_hbm, out_ref.at[pl.ds(0, mols), :], sems.at[0]),
        pltpu.make_async_copy(cols_hbm, cols_ref, sems.at[1]),
        pltpu.make_async_copy(count_hbm, count_ref, sems.at[2]),
    ]
    for load in loads:
        load.start()
    loads[1].wait()
    loads[2].wait()
    first = lax.axis_index("row") * blocks
    lane = lax.broadcasted_iota(jnp.int32, (TAIL, LANES), 1)
    row = lax.broadcasted_iota(jnp.int32, (TAIL, LANES), 0)
    table = jnp.zeros((TAIL, LANES), F32)
    for b in range(blocks):
        for s in range(slots):
            offset = jnp.where(s < count_ref[b], cols_ref[b, s] - (first + b) + BAND, -1)
            table = jnp.where(jnp.logical_and(lane == offset, row == b), 1.0, table)
    out_ref[pl.ds(mols, TAIL), :] = table.astype(BF16)
    loads[0].wait()


def compact(column):
    eye = lax.broadcasted_iota(jnp.int32, (LANES, LANES), 0) == lax.broadcasted_iota(jnp.int32, (LANES, LANES), 1)
    rows = []
    for k in range(column.shape[0] // LANES):
        rows.append(jnp.sum(jnp.where(eye, column[k * LANES : (k + 1) * LANES], 0.0), axis=0, keepdims=True))
    return jnp.concatenate(rows, axis=0)


def tile_weights(hl, b, e, w_ref, at, s_ref, diagonal):
    size, width = e.shape
    x = e.astype(F32)
    x = x * x
    high = x.astype(BF16)
    both = jnp.concatenate([high, (x - high.astype(F32)).astype(BF16)], axis=1)
    nt = (((1,), (1,)), ((), ()))
    total = lax.dot_general(jnp.ones((TAIL, 2 * width), BF16), both, nt, preferred_element_type=F32)
    inv = lax.rsqrt(total[0:1] * (1.0 / width) + EPS)
    ee = jnp.concatenate([e, e], axis=1)
    s_ref[...] = lax.dot_general(hl[pl.ds(b * size, size), :], ee, nt, preferred_element_type=F32)
    parts = []
    rows = 32
    for k in range(size // rows):
        w = jnp.exp2(s_ref[pl.ds(k * rows, rows), :] * inv - 2.0 * KERNEL_SCALE * LOG2E)
        if diagonal is not None:
            i = lax.broadcasted_iota(jnp.int32, (rows, size), 0) + k * rows
            j = lax.broadcasted_iota(jnp.int32, (rows, size), 1)
            w = jnp.where(jnp.logical_and(i == j, diagonal), 0.0, w)
        w_ref[at, pl.ds(k * rows, rows), :] = w.astype(BF16)
        parts.append(lanes_sum(w))
    return parts


def add_parts(ref, first, parts, mask, start):
    rows = parts[0].shape[0]
    for k, part in enumerate(parts):
        at = pl.ds(first + k * rows, rows)
        value = part * mask
        ref[at, :] = value if start else ref[at, :] + value


def own_weights_kernel(blocks, pack_ref, hl, w_ref, row_ref, col_ref, s_ref):
    mols = hl.shape[0]
    size, width = mols // blocks, hl.shape[1] // 2
    c = lax.axis_index("col")
    table = pack_ref[pl.ds(mols, TAIL), :].astype(F32)
    for b in range(blocks):
        x = pack_ref[pl.ds(b * size, size), :].astype(F32)
        scale = lax.rsqrt(jnp.sum(x * x, axis=-1, keepdims=True) * (1.0 / width) + EPS)
        x = x * (scale * (2.0 * KERNEL_SCALE * LOG2E / width))
        high = x.astype(BF16)
        hl[pl.ds(b * size, size), :width] = high
        hl[pl.ds(b * size, size), width:] = (x - high.astype(F32)).astype(BF16)
    e = pack_ref[pl.ds(pl.multiple_of(c * size, size), size), :]
    for b in range(blocks):
        parts = tile_weights(hl, b, e, w_ref, b, s_ref, c == b)
        from_c = jnp.where(c == 0, table_entry(table, 0, b), table_entry(table, 1, b - 1))
        add_parts(row_ref, b * size, parts, table_entry(table, b, c - b), True)
        add_parts(col_ref, b * size, parts, from_c, True)


def peer_weights_kernel(dims, offsets, pack_ref, peer_ref, hl, row_in, col_in, w_ref, *rest):
    blocks, last = dims
    if last:
        deg_ref, row_ref, col_ref, s_ref = rest
    else:
        row_ref, col_ref, s_ref = rest
    mols = hl.shape[0]
    size = mols // blocks
    chips = peer_offset(offsets)
    valid = jnp.where(chips != 0, 1.0, 0.0)
    own_table = pack_ref[pl.ds(mols, TAIL), :].astype(F32) * valid
    peer_table = peer_ref[pl.ds(mols, TAIL), :].astype(F32) * valid
    row_ref[...] = row_in[...]
    col_ref[...] = col_in[...]
    for k in range(blocks):
        e = peer_ref[pl.ds(k * size, size), :]
        for b in range(blocks):
            offset = chips * blocks + (k - b)
            parts = tile_weights(hl, b, e, w_ref, k * blocks + b, s_ref, None)
            add_parts(row_ref, b * size, parts, table_entry(own_table, b, offset), False)
            add_parts(col_ref, b * size, parts, table_entry(peer_table, k, -offset), False)
    if last:
        half = mols // LANES
        for n, ref in enumerate((row_ref, col_ref)):
            deg_ref[pl.ds(n * half, half), :] = compact(jnp.sum(ref[...], axis=-1, keepdims=True))


def seeds_kernel(mask_ref, profile_ref, after_ref, seed_ref, bf16_ref):
    del after_ref
    columns = mask_ref[...].astype(F32).T
    for k in range(mask_ref.shape[0]):
        at = pl.ds(k * LANES, LANES)
        seed = jnp.where(columns[:, k : k + 1] > 0.0, profile_ref[at, :], 0.0)
        seed_ref[at, :] = seed
        bf16_ref[at, :] = seed.astype(BF16)


def degree_kernel(own_ref, other_ref, out_ref):
    out_ref[...] = lax.rsqrt(own_ref[...] + other_ref[...])


def expand_kernel(scales_ref, seed_ref, scaled_ref, rs_ref, cs_ref):
    columns = scales_ref[...].T
    half = scales_ref.shape[0] // 2
    for k in range(half):
        at = pl.ds(k * LANES, LANES)
        by_col = jnp.broadcast_to(columns[:, half + k : half + k + 1], (LANES, LANES))
        rs_ref[at, :] = jnp.broadcast_to(columns[:, k : k + 1] * ALPHA, (LANES, LANES))
        cs_ref[at, :] = by_col
        scaled_ref[at, :] = (seed_ref[at, :] * by_col).astype(BF16)


def product_kernel(blocks, offsets, first, pack_ref, w_ref, scaled_ref, *rest):
    if first:
        scales_ref, _, out_ref, product_ref = rest
        columns = scales_ref[...].T
        half = scales_ref.shape[0] // 2
        for k in range(half):
            at = pl.ds(k * LANES, LANES)
            seed = scaled_ref[at, :].astype(F32)
            product_ref[at, :] = (seed * columns[:, half + k : half + k + 1]).astype(BF16)
        scaled_ref, rest = product_ref, rest[1:]
    else:
        out_ref = rest[-1]
    mols = scaled_ref.shape[0]
    size = mols // blocks
    table = pack_ref[pl.ds(mols, TAIL), :].astype(F32)
    c = lax.axis_index("col")
    if offsets is not None:
        chips = peer_offset(offsets)
        table = table * jnp.where(chips != 0, 1.0, 0.0)
    for b in range(blocks):
        at = pl.ds(b * size, size)
        if offsets is None:
            s = scaled_ref[pl.ds(pl.multiple_of(c * size, size), size), :].astype(F32)
            s = (s * table_entry(table, b, c - b)).astype(BF16)
            out_ref[at, :] = jnp.dot(w_ref[b], s, preferred_element_type=F32)
            continue
        total = rest[0][at, :]
        for k in range(blocks):
            offset = chips * blocks + (k - b)
            s = scaled_ref[pl.ds(k * size, size), :].astype(F32)
            s = (s * table_entry(table, b, offset)).astype(BF16)
            total = total + jnp.dot(w_ref[k * blocks + b], s, preferred_element_type=F32)
        out_ref[at, :] = total


def state_kernel(own_ref, other_ref, rs_ref, seed_ref, cs_ref, out_ref):
    state = (own_ref[...] + other_ref[...]) * rs_ref[...] + (1.0 - ALPHA) * seed_ref[...]
    out_ref[...] = (state * cs_ref[...]).astype(BF16)


def kernel_call(body, name, ins, outs, flops, scratch=(), in_specs=None):
    return pl.pallas_call(
        body,
        out_shape=outs,
        in_specs=in_specs or [VMEM] * len(ins),
        out_specs=jax.tree.map(lambda _: VMEM, outs),
        scratch_shapes=scratch,
        compiler_params=PARAMS,
        cost_estimate=pl.CostEstimate(flops=flops, bytes_accessed=1 << 20, transcendentals=0),
        name=name,
    )(*ins)


def shards(embeddings, profiles, seed_mask, tile_cols, tile_count):
    rows, cols = lax.axis_size("row"), lax.axis_size("col")
    blocks, slots = tile_cols.shape
    mols, width = embeddings.shape
    prof = profiles.shape[1]
    size = mols // blocks
    reach = (BAND + blocks - 1) // blocks
    assert blocks == 2 and cols == 2 and width == LANES and prof == LANES
    steps = exchange_steps(rows, cols, reach)
    f32_rows = jax.ShapeDtypeStruct((mols, LANES), F32)
    bf16_rows = jax.ShapeDtypeStruct((mols, LANES), BF16)
    tile_flops = 4 * size * size * width

    def to_peer(value, step):
        return lax.ppermute(value, ("row", "col"), list(steps[step][2].items()))

    def from_peers(value, forward=False):
        pieces = []
        for step, (moves, _, _) in enumerate(steps):
            if forward and step > 1:
                pieces.append(lax.ppermute(pieces[step - 2], ("row", "col"), list(moves.items())))
            else:
                pieces.append(to_peer(value, step))
        return pieces

    def other_core(value):
        return lax.ppermute(value, "col", [(0, 1), (1, 0)])

    def weights_of(tiles):
        return jax.ShapeDtypeStruct((tiles, size, size), BF16)

    chunks = mols // LANES
    held = [pltpu.with_memory_space_constraint(t, pltpu.HBM) for t in (embeddings, tile_cols, tile_count)]
    pack = kernel_call(
        lambda *refs: pack_kernel(blocks, slots, *refs),
        "pack",
        held,
        jax.ShapeDtypeStruct((mols + TAIL, LANES), BF16),
        1,
        [
            pltpu.SMEM(tile_cols.shape, jnp.int32),
            pltpu.SMEM(tile_count.shape, jnp.int32),
            pltpu.SemaphoreType.DMA((3,)),
        ],
        [HBM] * 3,
    )
    peer_packs = from_peers(pack, FORWARD[0])
    one_tile = pltpu.VMEM((size, size), F32)
    hl, own_weights, row_sum, col_sum = kernel_call(
        lambda *refs: own_weights_kernel(blocks, *refs),
        "own_weights",
        [pack],
        (jax.ShapeDtypeStruct((mols, 2 * width), BF16), weights_of(blocks), f32_rows, f32_rows),
        blocks * tile_flops,
        [one_tile],
    )
    weights = [own_weights] + [None] * len(steps)
    for rank, step in enumerate([1, 0, 2]):
        offsets = steps[step][1]
        last = rank + 1 == len(steps)
        if rank == 0:
            seed_rows, seeds = kernel_call(
                seeds_kernel, "seeds", [seed_mask.reshape(chunks, LANES), profiles, row_sum], (f32_rows, bf16_rows), 1
            )
            peer_seeds = from_peers(seeds, FORWARD[1])
        ins = [pack, peer_packs[step], hl, row_sum, col_sum]
        degrees = jax.ShapeDtypeStruct((2 * chunks, LANES), F32)
        out = kernel_call(
            lambda *refs, offsets=offsets, last=last: peer_weights_kernel((blocks, last), offsets, *refs),
            "peer_weights",
            ins,
            (weights_of(blocks * blocks), degrees) if last else (weights_of(blocks * blocks), f32_rows, f32_rows),
            blocks * blocks * tile_flops,
            [pltpu.VMEM((mols, LANES), F32)] * 2 + [one_tile] if last else [one_tile],
        )
        weights[1 + step] = out[0]
        if last:
            degree = out[1]
        else:
            row_sum, col_sum = out[1:]
    scales = kernel_call(degree_kernel, "degree", [degree, other_core(degree)], degrees, 1)
    peer_scales = [to_peer(scales, step) for step in range(len(steps) - 1)]
    held_scales, peer_seeds[0] = lax.optimization_barrier((scales, peer_seeds[0]))
    peer_scales.append(to_peer(held_scales, len(steps) - 1))
    scaled, row_scale, col_scale = kernel_call(
        expand_kernel, "expand", [scales, seed_rows], (bf16_rows, f32_rows, f32_rows), 1
    )
    for iteration in range(ITERS):
        first = iteration == 0
        peers = peer_seeds if first else from_peers(scaled, FORWARD[2])
        partial = kernel_call(
            lambda *refs: product_kernel(blocks, None, False, *refs),
            "own_product",
            [pack, weights[0], scaled],
            f32_rows,
            blocks * tile_flops,
        )
        for step in [1, 0, 2]:
            offsets = steps[step][1]
            partial = kernel_call(
                lambda *refs, offsets=offsets, first=first: product_kernel(blocks, offsets, first, *refs),
                "peer_product",
                [pack, weights[1 + step], peers[step]] + [peer_scales[step]] * first + [partial],
                f32_rows,
                blocks * blocks * tile_flops,
                [pltpu.VMEM((mols, LANES), BF16)] * first,
            )
        other = other_core(partial)
        if iteration + 1 < ITERS:
            scaled = kernel_call(
                state_kernel, "state", [partial, other, row_scale, seed_rows, col_scale], bf16_rows, 1
            )
    return (partial + other) * row_scale + (1.0 - ALPHA) * seed_rows


def solution(mesh):
    placed = (
        P(("grp", "row"), None),
        P(("grp", "row"), None),
        P(("grp", "row")),
        P(("grp", "row"), None),
        P(("grp", "row")),
    )
    return jax.shard_map(
        shards, mesh=mesh, in_specs=placed, out_specs=P(("grp", "row"), None), check_vma=False
    )
```

```python
import jax
import jax.numpy as jnp
from jax import lax
from jax.experimental import pallas as pl
from jax.experimental.pallas import tpu as pltpu
from jax.sharding import PartitionSpec as P

BAND = 6
ITERS = 2

KERNEL_SCALE = 12.5
ALPHA = 0.8
EPS = 1e-06
LOG2E = 1.4426950408889634
LANES = 128
TAIL = 16
F32 = jnp.float32
BF16 = jnp.bfloat16

VMEM = pl.BlockSpec(memory_space=pltpu.VMEM)
HBM = pl.BlockSpec(memory_space=pltpu.HBM)
PARAMS = pltpu.CompilerParams(vmem_limit_bytes=24 * 1024 * 1024)


FORWARD = (True, True, True)


def distance_of(chip, device, cols):
    return abs(chip - device // cols)


def complete(moves, rows, cols, fixed):
    moves = dict(moves)
    sources = [n for n in range(rows * cols) if n not in moves]
    targets = [n for n in range(rows * cols) if n not in moves.values()]
    for s in list(sources):
        other = [t for t in targets if t // cols == s // cols and t != s]
        if other:
            moves[s] = other[0]
            sources.remove(s)
            targets.remove(other[0])
    for s in list(sources):
        if s in targets:
            y = s ^ 1
            if fixed:
                moves[s] = moves[y]
                moves[y] = s
            else:
                z = next(n for n, t in moves.items() if t == y)
                moves[z] = s
                moves[s] = y
            sources.remove(s)
            targets.remove(s)
    for s, t in zip(sources, targets):
        moves[s] = t
    return moves


def landings(moves, origin, rows, cols, distance):
    table = [[0] * rows for _ in range(cols)]
    for s, t in moves.items():
        if origin(s) is not None and distance_of(origin(s), t, cols) == distance:
            table[t % cols][t // cols] = origin(s) - t // cols
    return table


def exchange_steps(rows, cols, reach):
    steps = []
    for d in range(1, reach + 1):
        if d < 3:
            moves = {}
            for a in range(rows - d):
                core = a // d % cols
                moves[a * cols + core] = (a + d) * cols + core
                moves[(a + d) * cols + core] = a * cols + core
            moves = complete(moves, rows, cols, False)
            table = landings(moves, lambda s: s // cols, rows, cols, d)
            steps.append((moves, table, moves))
            continue
        held = steps[d - 3][1]

        def origin(s, held=held):
            offset = held[s % cols][s // cols]
            return s // cols + offset if offset else None

        moves, taken = {}, [0] * rows
        for s in range(rows * cols):
            if origin(s) is not None:
                t = s // cols + (2 if origin(s) < s // cols else -2)
                if 0 <= t < rows:
                    moves[s] = t * cols + taken[t]
                    taken[t] += 1
        moves = complete(moves, rows, cols, False)
        table = landings(moves, origin, rows, cols, d)
        direct, sent = {}, [0] * rows
        for chip in range(rows):
            for core in range(cols):
                if table[core][chip]:
                    source = chip + table[core][chip]
                    direct[source * cols + sent[source]] = chip * cols + core
                    sent[source] += 1
        direct = complete(direct, rows, cols, True)
        steps.append((moves, table, direct))
    return steps


def peer_offset(offsets):
    r, c = lax.axis_index("row"), lax.axis_index("col")
    value = jnp.int32(0)
    for core, per_row in enumerate(offsets):
        for word, first in enumerate(range(0, len(per_row), 8)):
            code = sum((offset + 8) << (4 * n) for n, offset in enumerate(per_row[first : first + 8]))
            code = jnp.int32(code - (1 << 32) if code >= 1 << 31 else code)
            digit = (lax.shift_right_logical(code, 4 * lax.rem(r, 8)) & 15) - 8
            here = jnp.logical_and(c == core, lax.div(r, 8) == word)
            value = jnp.where(here, digit, value)
    return value


def table_entry(table, row, offset):
    lane = lax.broadcasted_iota(jnp.int32, (1, LANES), 1)
    return jnp.max(jnp.where(lane == offset + BAND, table[row : row + 1, :], 0.0), axis=-1, keepdims=True)


def lanes_sum(w):
    part = w[:, :LANES]
    for k in range(1, w.shape[1] // LANES):
        part = part + w[:, k * LANES : (k + 1) * LANES]
    return part


def pack_kernel(blocks, slots, emb_hbm, cols_hbm, count_hbm, out_ref, cols_ref, count_ref, sems):
    mols = emb_hbm.shape[0]
    loads = [
        pltpu.make_async_copy(emb_hbm, out_ref.at[pl.ds(0, mols), :], sems.at[0]),
        pltpu.make_async_copy(cols_hbm, cols_ref, sems.at[1]),
        pltpu.make_async_copy(count_hbm, count_ref, sems.at[2]),
    ]
    for load in loads:
        load.start()
    loads[1].wait()
    loads[2].wait()
    first = lax.axis_index("row") * blocks
    lane = lax.broadcasted_iota(jnp.int32, (TAIL, LANES), 1)
    row = lax.broadcasted_iota(jnp.int32, (TAIL, LANES), 0)
    table = jnp.zeros((TAIL, LANES), F32)
    for b in range(blocks):
        for s in range(slots):
            offset = jnp.where(s < count_ref[b], cols_ref[b, s] - (first + b) + BAND, -1)
            table = jnp.where(jnp.logical_and(lane == offset, row == b), 1.0, table)
    out_ref[pl.ds(mols, TAIL), :] = table.astype(BF16)
    loads[0].wait()


def compact(column):
    eye = lax.broadcasted_iota(jnp.int32, (LANES, LANES), 0) == lax.broadcasted_iota(jnp.int32, (LANES, LANES), 1)
    rows = []
    for k in range(column.shape[0] // LANES):
        rows.append(jnp.sum(jnp.where(eye, column[k * LANES : (k + 1) * LANES], 0.0), axis=0, keepdims=True))
    return jnp.concatenate(rows, axis=0)


def tile_weights(hl, b, e, w_ref, at, s_ref, diagonal):
    size, width = e.shape
    x = e.astype(F32)
    x = x * x
    high = x.astype(BF16)
    both = jnp.concatenate([high, (x - high.astype(F32)).astype(BF16)], axis=1)
    nt = (((1,), (1,)), ((), ()))
    total = lax.dot_general(jnp.ones((TAIL, 2 * width), BF16), both, nt, preferred_element_type=F32)
    inv = lax.rsqrt(total[0:1] * (1.0 / width) + EPS)
    ee = jnp.concatenate([e, e], axis=1)
    s_ref[...] = lax.dot_general(hl[pl.ds(b * size, size), :], ee, nt, preferred_element_type=F32)
    parts = []
    rows = 32
    for k in range(size // rows):
        w = jnp.exp2(s_ref[pl.ds(k * rows, rows), :] * inv - 2.0 * KERNEL_SCALE * LOG2E)
        if diagonal is not None:
            i = lax.broadcasted_iota(jnp.int32, (rows, size), 0) + k * rows
            j = lax.broadcasted_iota(jnp.int32, (rows, size), 1)
            w = jnp.where(jnp.logical_and(i == j, diagonal), 0.0, w)
        w_ref[at, pl.ds(k * rows, rows), :] = w.astype(BF16)
        parts.append(lanes_sum(w))
    return parts


def add_parts(ref, first, parts, mask, start):
    rows = parts[0].shape[0]
    for k, part in enumerate(parts):
        at = pl.ds(first + k * rows, rows)
        value = part * mask
        ref[at, :] = value if start else ref[at, :] + value


def own_weights_kernel(blocks, pack_ref, hl, w_ref, row_ref, col_ref, s_ref):
    mols = hl.shape[0]
    size, width = mols // blocks, hl.shape[1] // 2
    c = lax.axis_index("col")
    table = pack_ref[pl.ds(mols, TAIL), :].astype(F32)
    for b in range(blocks):
        x = pack_ref[pl.ds(b * size, size), :].astype(F32)
        scale = lax.rsqrt(jnp.sum(x * x, axis=-1, keepdims=True) * (1.0 / width) + EPS)
        x = x * (scale * (2.0 * KERNEL_SCALE * LOG2E / width))
        high = x.astype(BF16)
        hl[pl.ds(b * size, size), :width] = high
        hl[pl.ds(b * size, size), width:] = (x - high.astype(F32)).astype(BF16)
    e = pack_ref[pl.ds(pl.multiple_of(c * size, size), size), :]
    for b in range(blocks):
        parts = tile_weights(hl, b, e, w_ref, b, s_ref, c == b)
        from_c = jnp.where(c == 0, table_entry(table, 0, b), table_entry(table, 1, b - 1))
        add_parts(row_ref, b * size, parts, table_entry(table, b, c - b), True)
        add_parts(col_ref, b * size, parts, from_c, True)


def peer_weights_kernel(dims, offsets, pack_ref, peer_ref, hl, row_in, col_in, w_ref, *rest):
    blocks, last = dims
    if last:
        deg_ref, row_ref, col_ref, s_ref = rest
    else:
        row_ref, col_ref, s_ref = rest
    mols = hl.shape[0]
    size = mols // blocks
    chips = peer_offset(offsets)
    valid = jnp.where(chips != 0, 1.0, 0.0)
    own_table = pack_ref[pl.ds(mols, TAIL), :].astype(F32) * valid
    peer_table = peer_ref[pl.ds(mols, TAIL), :].astype(F32) * valid
    row_ref[...] = row_in[...]
    col_ref[...] = col_in[...]
    for k in range(blocks):
        e = peer_ref[pl.ds(k * size, size), :]
        for b in range(blocks):
            offset = chips * blocks + (k - b)
            parts = tile_weights(hl, b, e, w_ref, k * blocks + b, s_ref, None)
            add_parts(row_ref, b * size, parts, table_entry(own_table, b, offset), False)
            add_parts(col_ref, b * size, parts, table_entry(peer_table, k, -offset), False)
    if last:
        half = mols // LANES
        for n, ref in enumerate((row_ref, col_ref)):
            deg_ref[pl.ds(n * half, half), :] = compact(jnp.sum(ref[...], axis=-1, keepdims=True))


def seeds_kernel(mask_ref, profile_ref, after_ref, seed_ref, bf16_ref):
    del after_ref
    columns = mask_ref[...].astype(F32).T
    for k in range(mask_ref.shape[0]):
        at = pl.ds(k * LANES, LANES)
        seed = jnp.where(columns[:, k : k + 1] > 0.0, profile_ref[at, :], 0.0)
        seed_ref[at, :] = seed
        bf16_ref[at, :] = seed.astype(BF16)


def degree_kernel(own_ref, other_ref, out_ref):
    out_ref[...] = lax.rsqrt(own_ref[...] + other_ref[...])


def expand_kernel(scales_ref, seed_ref, scaled_ref, rs_ref, cs_ref):
    columns = scales_ref[...].T
    half = scales_ref.shape[0] // 2
    for k in range(half):
        at = pl.ds(k * LANES, LANES)
        by_col = jnp.broadcast_to(columns[:, half + k : half + k + 1], (LANES, LANES))
        rs_ref[at, :] = jnp.broadcast_to(columns[:, k : k + 1] * ALPHA, (LANES, LANES))
        cs_ref[at, :] = by_col
        scaled_ref[at, :] = (seed_ref[at, :] * by_col).astype(BF16)


def product_kernel(blocks, offsets, first, pack_ref, w_ref, scaled_ref, *rest):
    if first:
        scales_ref, _, out_ref, product_ref = rest
        columns = scales_ref[...].T
        half = scales_ref.shape[0] // 2
        for k in range(half):
            at = pl.ds(k * LANES, LANES)
            seed = scaled_ref[at, :].astype(F32)
            product_ref[at, :] = (seed * columns[:, half + k : half + k + 1]).astype(BF16)
        scaled_ref, rest = product_ref, rest[1:]
    else:
        out_ref = rest[-1]
    mols = scaled_ref.shape[0]
    size = mols // blocks
    table = pack_ref[pl.ds(mols, TAIL), :].astype(F32)
    c = lax.axis_index("col")
    if offsets is not None:
        chips = peer_offset(offsets)
        table = table * jnp.where(chips != 0, 1.0, 0.0)
    for b in range(blocks):
        at = pl.ds(b * size, size)
        if offsets is None:
            s = scaled_ref[pl.ds(pl.multiple_of(c * size, size), size), :].astype(F32)
            s = (s * table_entry(table, b, c - b)).astype(BF16)
            out_ref[at, :] = jnp.dot(w_ref[b], s, preferred_element_type=F32)
            continue
        total = rest[0][at, :]
        for k in range(blocks):
            offset = chips * blocks + (k - b)
            s = scaled_ref[pl.ds(k * size, size), :].astype(F32)
            s = (s * table_entry(table, b, offset)).astype(BF16)
            total = total + jnp.dot(w_ref[k * blocks + b], s, preferred_element_type=F32)
        out_ref[at, :] = total.astype(out_ref.dtype)


def state_kernel(own_ref, other_ref, rs_ref, seed_ref, cs_ref, out_ref):
    state = (own_ref[...].astype(F32) + other_ref[...].astype(F32)) * rs_ref[...] + (1.0 - ALPHA) * seed_ref[...]
    out_ref[...] = (state * cs_ref[...]).astype(BF16)


def kernel_call(body, name, ins, outs, flops, scratch=(), in_specs=None):
    return pl.pallas_call(
        body,
        out_shape=outs,
        in_specs=in_specs or [VMEM] * len(ins),
        out_specs=jax.tree.map(lambda _: VMEM, outs),
        scratch_shapes=scratch,
        compiler_params=PARAMS,
        cost_estimate=pl.CostEstimate(flops=flops, bytes_accessed=1 << 20, transcendentals=0),
        name=name,
    )(*ins)


def shards(embeddings, profiles, seed_mask, tile_cols, tile_count):
    rows, cols = lax.axis_size("row"), lax.axis_size("col")
    blocks, slots = tile_cols.shape
    mols, width = embeddings.shape
    prof = profiles.shape[1]
    size = mols // blocks
    reach = (BAND + blocks - 1) // blocks
    assert blocks == 2 and cols == 2 and width == LANES and prof == LANES
    steps = exchange_steps(rows, cols, reach)
    f32_rows = jax.ShapeDtypeStruct((mols, LANES), F32)
    bf16_rows = jax.ShapeDtypeStruct((mols, LANES), BF16)
    tile_flops = 4 * size * size * width

    def to_peer(value, step):
        return lax.ppermute(value, ("row", "col"), list(steps[step][2].items()))

    def from_peers(value, forward=False):
        pieces = []
        for step, (moves, _, _) in enumerate(steps):
            if forward and step > 1:
                pieces.append(lax.ppermute(pieces[step - 2], ("row", "col"), list(moves.items())))
            else:
                pieces.append(to_peer(value, step))
        return pieces

    def other_core(value):
        return lax.ppermute(value, "col", [(0, 1), (1, 0)])

    def weights_of(tiles):
        return jax.ShapeDtypeStruct((tiles, size, size), BF16)

    chunks = mols // LANES
    held = [pltpu.with_memory_space_constraint(t, pltpu.HBM) for t in (embeddings, tile_cols, tile_count)]
    pack = kernel_call(
        lambda *refs: pack_kernel(blocks, slots, *refs),
        "pack",
        held,
        jax.ShapeDtypeStruct((mols + TAIL, LANES), BF16),
        1,
        [
            pltpu.SMEM(tile_cols.shape, jnp.int32),
            pltpu.SMEM(tile_count.shape, jnp.int32),
            pltpu.SemaphoreType.DMA((3,)),
        ],
        [HBM] * 3,
    )
    peer_packs = from_peers(pack, FORWARD[0])
    one_tile = pltpu.VMEM((size, size), F32)
    hl, own_weights, row_sum, col_sum = kernel_call(
        lambda *refs: own_weights_kernel(blocks, *refs),
        "own_weights",
        [pack],
        (jax.ShapeDtypeStruct((mols, 2 * width), BF16), weights_of(blocks), f32_rows, f32_rows),
        blocks * tile_flops,
        [one_tile],
    )
    weights = [own_weights] + [None] * len(steps)
    for rank, step in enumerate([1, 0, 2]):
        offsets = steps[step][1]
        last = rank + 1 == len(steps)
        if rank == 0:
            seed_rows, seeds = kernel_call(
                seeds_kernel, "seeds", [seed_mask.reshape(chunks, LANES), profiles, row_sum], (f32_rows, bf16_rows), 1
            )
            peer_seeds = from_peers(seeds, FORWARD[1])
        ins = [pack, peer_packs[step], hl, row_sum, col_sum]
        degrees = jax.ShapeDtypeStruct((2 * chunks, LANES), F32)
        out = kernel_call(
            lambda *refs, offsets=offsets, last=last: peer_weights_kernel((blocks, last), offsets, *refs),
            "peer_weights",
            ins,
            (weights_of(blocks * blocks), degrees) if last else (weights_of(blocks * blocks), f32_rows, f32_rows),
            blocks * blocks * tile_flops,
            [pltpu.VMEM((mols, LANES), F32)] * 2 + [one_tile] if last else [one_tile],
        )
        weights[1 + step] = out[0]
        if last:
            degree = out[1]
        else:
            row_sum, col_sum = out[1:]
    scales = kernel_call(degree_kernel, "degree", [degree, other_core(degree)], degrees, 1)
    peer_scales = [to_peer(scales, step) for step in range(len(steps) - 1)]
    held_scales, peer_seeds[0] = lax.optimization_barrier((scales, peer_seeds[0]))
    peer_scales.append(to_peer(held_scales, len(steps) - 1))
    scaled, row_scale, col_scale = kernel_call(
        expand_kernel, "expand", [scales, seed_rows], (bf16_rows, f32_rows, f32_rows), 1
    )
    for iteration in range(ITERS):
        first = iteration == 0
        peers = peer_seeds if first else from_peers(scaled, FORWARD[2])
        partial = kernel_call(
            lambda *refs: product_kernel(blocks, None, False, *refs),
            "own_product",
            [pack, weights[0], scaled],
            f32_rows,
            blocks * tile_flops,
        )
        for step in [1, 0, 2]:
            offsets = steps[step][1]
            final = step + 1 == len(steps)
            partial = kernel_call(
                lambda *refs, offsets=offsets, first=first: product_kernel(blocks, offsets, first, *refs),
                "peer_product",
                [pack, weights[1 + step], peers[step]] + [peer_scales[step]] * first + [partial],
                bf16_rows if final else f32_rows,
                blocks * blocks * tile_flops,
                [pltpu.VMEM((mols, LANES), BF16)] * first,
            )
        other = other_core(partial)
        if iteration + 1 < ITERS:
            scaled = kernel_call(
                state_kernel, "state", [partial, other, row_scale, seed_rows, col_scale], bf16_rows, 1
            )
    return (partial.astype(F32) + other.astype(F32)) * row_scale + (1.0 - ALPHA) * seed_rows


def solution(mesh):
    placed = (
        P(("grp", "row"), None),
        P(("grp", "row"), None),
        P(("grp", "row")),
        P(("grp", "row"), None),
        P(("grp", "row")),
    )
    return jax.shard_map(
        shards, mesh=mesh, in_specs=placed, out_specs=P(("grp", "row"), None), check_vma=False
    )
```

```python
import jax
import jax.numpy as jnp
from jax import lax
from jax.experimental import pallas as pl
from jax.experimental.pallas import tpu as pltpu
from jax.sharding import PartitionSpec as P

BAND = 6
ITERS = 2

KERNEL_SCALE = 12.5
ALPHA = 0.8
EPS = 1e-06
LOG2E = 1.4426950408889634
LANES = 128
TAIL = 16
F32 = jnp.float32
BF16 = jnp.bfloat16

VMEM = pl.BlockSpec(memory_space=pltpu.VMEM)
HBM = pl.BlockSpec(memory_space=pltpu.HBM)
PARAMS = pltpu.CompilerParams(vmem_limit_bytes=24 * 1024 * 1024)


FORWARD = (True, True, True)


def distance_of(chip, device, cols):
    return abs(chip - device // cols)


def complete(moves, rows, cols, fixed):
    moves = dict(moves)
    sources = [n for n in range(rows * cols) if n not in moves]
    targets = [n for n in range(rows * cols) if n not in moves.values()]
    for s in list(sources):
        other = [t for t in targets if t // cols == s // cols and t != s]
        if other:
            moves[s] = other[0]
            sources.remove(s)
            targets.remove(other[0])
    for s in list(sources):
        if s in targets:
            y = s ^ 1
            if fixed:
                moves[s] = moves[y]
                moves[y] = s
            else:
                z = next(n for n, t in moves.items() if t == y)
                moves[z] = s
                moves[s] = y
            sources.remove(s)
            targets.remove(s)
    for s, t in zip(sources, targets):
        moves[s] = t
    return moves


def landings(moves, origin, rows, cols, distance):
    table = [[0] * rows for _ in range(cols)]
    for s, t in moves.items():
        if origin(s) is not None and distance_of(origin(s), t, cols) == distance:
            table[t % cols][t // cols] = origin(s) - t // cols
    return table


def exchange_steps(rows, cols, reach):
    steps = []
    for d in range(1, reach + 1):
        if d < 3:
            moves = {}
            for a in range(rows - d):
                core = a // d % cols
                moves[a * cols + core] = (a + d) * cols + core
                moves[(a + d) * cols + core] = a * cols + core
            moves = complete(moves, rows, cols, False)
            table = landings(moves, lambda s: s // cols, rows, cols, d)
            steps.append((moves, table, moves))
            continue
        held = steps[d - 3][1]

        def origin(s, held=held):
            offset = held[s % cols][s // cols]
            return s // cols + offset if offset else None

        moves, taken = {}, [0] * rows
        for s in range(rows * cols):
            if origin(s) is not None:
                t = s // cols + (2 if origin(s) < s // cols else -2)
                if 0 <= t < rows:
                    moves[s] = t * cols + taken[t]
                    taken[t] += 1
        moves = complete(moves, rows, cols, False)
        table = landings(moves, origin, rows, cols, d)
        direct, sent = {}, [0] * rows
        for chip in range(rows):
            for core in range(cols):
                if table[core][chip]:
                    source = chip + table[core][chip]
                    direct[source * cols + sent[source]] = chip * cols + core
                    sent[source] += 1
        direct = complete(direct, rows, cols, True)
        steps.append((moves, table, direct))
    return steps


def peer_offset(offsets):
    r, c = lax.axis_index("row"), lax.axis_index("col")
    value = jnp.int32(0)
    for core, per_row in enumerate(offsets):
        for word, first in enumerate(range(0, len(per_row), 8)):
            code = sum((offset + 8) << (4 * n) for n, offset in enumerate(per_row[first : first + 8]))
            code = jnp.int32(code - (1 << 32) if code >= 1 << 31 else code)
            digit = (lax.shift_right_logical(code, 4 * lax.rem(r, 8)) & 15) - 8
            here = jnp.logical_and(c == core, lax.div(r, 8) == word)
            value = jnp.where(here, digit, value)
    return value


def table_entry(table, row, offset):
    lane = lax.broadcasted_iota(jnp.int32, (1, LANES), 1)
    return jnp.max(jnp.where(lane == offset + BAND, table[row : row + 1, :], 0.0), axis=-1, keepdims=True)


def lanes_sum(w):
    part = w[:, :LANES]
    for k in range(1, w.shape[1] // LANES):
        part = part + w[:, k * LANES : (k + 1) * LANES]
    return part


def pack_kernel(blocks, slots, emb_hbm, cols_hbm, count_hbm, out_ref, cols_ref, count_ref, sems):
    mols = emb_hbm.shape[0]
    loads = [
        pltpu.make_async_copy(emb_hbm, out_ref.at[pl.ds(0, mols), :], sems.at[0]),
        pltpu.make_async_copy(cols_hbm, cols_ref, sems.at[1]),
        pltpu.make_async_copy(count_hbm, count_ref, sems.at[2]),
    ]
    for load in loads:
        load.start()
    loads[1].wait()
    loads[2].wait()
    first = lax.axis_index("row") * blocks
    lane = lax.broadcasted_iota(jnp.int32, (TAIL, LANES), 1)
    row = lax.broadcasted_iota(jnp.int32, (TAIL, LANES), 0)
    table = jnp.zeros((TAIL, LANES), F32)
    for b in range(blocks):
        for s in range(slots):
            offset = jnp.where(s < count_ref[b], cols_ref[b, s] - (first + b) + BAND, -1)
            table = jnp.where(jnp.logical_and(lane == offset, row == b), 1.0, table)
    out_ref[pl.ds(mols, TAIL), :] = table.astype(BF16)
    loads[0].wait()


def compact(column):
    eye = lax.broadcasted_iota(jnp.int32, (LANES, LANES), 0) == lax.broadcasted_iota(jnp.int32, (LANES, LANES), 1)
    rows = []
    for k in range(column.shape[0] // LANES):
        rows.append(jnp.sum(jnp.where(eye, column[k * LANES : (k + 1) * LANES], 0.0), axis=0, keepdims=True))
    return jnp.concatenate(rows, axis=0)


def tile_weights(hl, b, e, w_ref, at, s_ref, diagonal):
    size, width = e.shape
    x = e.astype(F32)
    x = x * x
    high = x.astype(BF16)
    both = jnp.concatenate([high, (x - high.astype(F32)).astype(BF16)], axis=1)
    nt = (((1,), (1,)), ((), ()))
    total = lax.dot_general(jnp.ones((TAIL, 2 * width), BF16), both, nt, preferred_element_type=F32)
    inv = lax.rsqrt(total[0:1] * (1.0 / width) + EPS)
    ee = jnp.concatenate([e, e], axis=1)
    s_ref[...] = lax.dot_general(hl[pl.ds(b * size, size), :], ee, nt, preferred_element_type=F32)
    parts = []
    rows = 32
    for k in range(size // rows):
        w = jnp.exp2(s_ref[pl.ds(k * rows, rows), :] * inv - 2.0 * KERNEL_SCALE * LOG2E)
        if diagonal is not None:
            i = lax.broadcasted_iota(jnp.int32, (rows, size), 0) + k * rows
            j = lax.broadcasted_iota(jnp.int32, (rows, size), 1)
            w = jnp.where(jnp.logical_and(i == j, diagonal), 0.0, w)
        w_ref[at, pl.ds(k * rows, rows), :] = w.astype(BF16)
        parts.append(lanes_sum(w))
    return parts


def add_parts(ref, first, parts, mask, start):
    rows = parts[0].shape[0]
    for k, part in enumerate(parts):
        at = pl.ds(first + k * rows, rows)
        value = part * mask
        ref[at, :] = value if start else ref[at, :] + value


def own_weights_kernel(blocks, pack_ref, hl, w_ref, row_ref, col_ref, s_ref):
    mols = hl.shape[0]
    size, width = mols // blocks, hl.shape[1] // 2
    c = lax.axis_index("col")
    table = pack_ref[pl.ds(mols, TAIL), :].astype(F32)
    for b in range(blocks):
        x = pack_ref[pl.ds(b * size, size), :].astype(F32)
        scale = lax.rsqrt(jnp.sum(x * x, axis=-1, keepdims=True) * (1.0 / width) + EPS)
        x = x * (scale * (2.0 * KERNEL_SCALE * LOG2E / width))
        high = x.astype(BF16)
        hl[pl.ds(b * size, size), :width] = high
        hl[pl.ds(b * size, size), width:] = (x - high.astype(F32)).astype(BF16)
    e = pack_ref[pl.ds(pl.multiple_of(c * size, size), size), :]
    for b in range(blocks):
        parts = tile_weights(hl, b, e, w_ref, b, s_ref, c == b)
        from_c = jnp.where(c == 0, table_entry(table, 0, b), table_entry(table, 1, b - 1))
        add_parts(row_ref, b * size, parts, table_entry(table, b, c - b), True)
        add_parts(col_ref, b * size, parts, from_c, True)


def peer_weights_kernel(dims, offsets, pack_ref, peer_ref, hl, row_in, col_in, w_ref, *rest):
    blocks, last = dims
    if last:
        deg_ref, row_ref, col_ref, s_ref = rest
    else:
        row_ref, col_ref, s_ref = rest
    mols = hl.shape[0]
    size = mols // blocks
    chips = peer_offset(offsets)
    valid = jnp.where(chips != 0, 1.0, 0.0)
    own_table = pack_ref[pl.ds(mols, TAIL), :].astype(F32) * valid
    peer_table = peer_ref[pl.ds(mols, TAIL), :].astype(F32) * valid
    row_ref[...] = row_in[...]
    col_ref[...] = col_in[...]
    for k in range(blocks):
        e = peer_ref[pl.ds(k * size, size), :]
        for b in range(blocks):
            offset = chips * blocks + (k - b)
            parts = tile_weights(hl, b, e, w_ref, k * blocks + b, s_ref, None)
            add_parts(row_ref, b * size, parts, table_entry(own_table, b, offset), False)
            add_parts(col_ref, b * size, parts, table_entry(peer_table, k, -offset), False)
    if last:
        half = mols // LANES
        for n, ref in enumerate((row_ref, col_ref)):
            deg_ref[pl.ds(n * half, half), :] = compact(jnp.sum(ref[...], axis=-1, keepdims=True))


def seeds_kernel(mask_ref, profile_ref, after_ref, seed_ref, bf16_ref):
    del after_ref
    columns = mask_ref[...].astype(F32).T
    for k in range(mask_ref.shape[0]):
        at = pl.ds(k * LANES, LANES)
        seed = jnp.where(columns[:, k : k + 1] > 0.0, profile_ref[at, :], 0.0)
        seed_ref[at, :] = seed
        bf16_ref[at, :] = seed.astype(BF16)


def degree_kernel(own_ref, other_ref, out_ref):
    out_ref[...] = lax.rsqrt(own_ref[...] + other_ref[...])


def expand_kernel(scales_ref, seed_ref, scaled_ref, rs_ref, cs_ref):
    columns = scales_ref[...].T
    half = scales_ref.shape[0] // 2
    for k in range(half):
        at = pl.ds(k * LANES, LANES)
        by_col = jnp.broadcast_to(columns[:, half + k : half + k + 1], (LANES, LANES))
        rs_ref[at, :] = jnp.broadcast_to(columns[:, k : k + 1] * ALPHA, (LANES, LANES))
        cs_ref[at, :] = by_col
        scaled_ref[at, :] = (seed_ref[at, :] * by_col).astype(BF16)


def product_kernel(blocks, offsets, first, pack_ref, w_ref, scaled_ref, *rest):
    if first:
        scales_ref, _, out_ref, product_ref = rest
        columns = scales_ref[...].T
        half = scales_ref.shape[0] // 2
        for k in range(half):
            at = pl.ds(k * LANES, LANES)
            seed = scaled_ref[at, :].astype(F32)
            product_ref[at, :] = (seed * columns[:, half + k : half + k + 1]).astype(BF16)
        scaled_ref, rest = product_ref, rest[1:]
    else:
        out_ref = rest[-1]
    mols = scaled_ref.shape[0]
    size = mols // blocks
    table = pack_ref[pl.ds(mols, TAIL), :].astype(F32)
    c = lax.axis_index("col")
    if offsets is not None:
        chips = peer_offset(offsets)
        table = table * jnp.where(chips != 0, 1.0, 0.0)
    for b in range(blocks):
        at = pl.ds(b * size, size)
        if offsets is None:
            s = scaled_ref[pl.ds(pl.multiple_of(c * size, size), size), :].astype(F32)
            s = (s * table_entry(table, b, c - b)).astype(BF16)
            out_ref[at, :] = jnp.dot(w_ref[b], s, preferred_element_type=F32)
            continue
        total = rest[0][at, :]
        for k in range(blocks):
            offset = chips * blocks + (k - b)
            s = scaled_ref[pl.ds(k * size, size), :].astype(F32)
            s = (s * table_entry(table, b, offset)).astype(BF16)
            total = total + jnp.dot(w_ref[k * blocks + b], s, preferred_element_type=F32)
        out_ref[at, :] = total.astype(out_ref.dtype)


def state_kernel(own_ref, other_ref, rs_ref, seed_ref, cs_ref, out_ref):
    state = (own_ref[...].astype(F32) + other_ref[...].astype(F32)) * rs_ref[...] + (1.0 - ALPHA) * seed_ref[...]
    out_ref[...] = (state * cs_ref[...]).astype(BF16)


def kernel_call(body, name, ins, outs, flops, scratch=(), in_specs=None):
    return pl.pallas_call(
        body,
        out_shape=outs,
        in_specs=in_specs or [VMEM] * len(ins),
        out_specs=jax.tree.map(lambda _: VMEM, outs),
        scratch_shapes=scratch,
        compiler_params=PARAMS,
        cost_estimate=pl.CostEstimate(flops=flops, bytes_accessed=1 << 20, transcendentals=0),
        name=name,
    )(*ins)


def shards(embeddings, profiles, seed_mask, tile_cols, tile_count):
    rows, cols = lax.axis_size("row"), lax.axis_size("col")
    blocks, slots = tile_cols.shape
    mols, width = embeddings.shape
    prof = profiles.shape[1]
    size = mols // blocks
    reach = (BAND + blocks - 1) // blocks
    assert blocks == 2 and cols == 2 and width == LANES and prof == LANES
    steps = exchange_steps(rows, cols, reach)
    f32_rows = jax.ShapeDtypeStruct((mols, LANES), F32)
    bf16_rows = jax.ShapeDtypeStruct((mols, LANES), BF16)
    tile_flops = 4 * size * size * width

    def to_peer(value, step):
        return lax.ppermute(value, ("row", "col"), list(steps[step][2].items()))

    def from_peers(value, forward=False):
        pieces = []
        for step, (moves, _, _) in enumerate(steps):
            if forward and step > 1:
                pieces.append(lax.ppermute(pieces[step - 2], ("row", "col"), list(moves.items())))
            else:
                pieces.append(to_peer(value, step))
        return pieces

    def other_core(value):
        return lax.ppermute(value, "col", [(0, 1), (1, 0)])

    def weights_of(tiles):
        return jax.ShapeDtypeStruct((tiles, size, size), BF16)

    chunks = mols // LANES
    held = [pltpu.with_memory_space_constraint(t, pltpu.HBM) for t in (embeddings, tile_cols, tile_count)]
    pack = kernel_call(
        lambda *refs: pack_kernel(blocks, slots, *refs),
        "pack",
        held,
        jax.ShapeDtypeStruct((mols + TAIL, LANES), BF16),
        1,
        [
            pltpu.SMEM(tile_cols.shape, jnp.int32),
            pltpu.SMEM(tile_count.shape, jnp.int32),
            pltpu.SemaphoreType.DMA((3,)),
        ],
        [HBM] * 3,
    )
    peer_packs = from_peers(pack, FORWARD[0])
    one_tile = pltpu.VMEM((size, size), F32)
    hl, own_weights, row_sum, col_sum = kernel_call(
        lambda *refs: own_weights_kernel(blocks, *refs),
        "own_weights",
        [pack],
        (jax.ShapeDtypeStruct((mols, 2 * width), BF16), weights_of(blocks), f32_rows, f32_rows),
        blocks * tile_flops,
        [one_tile],
    )
    weights = [own_weights] + [None] * len(steps)
    for rank, step in enumerate([1, 0, 2]):
        offsets = steps[step][1]
        last = rank + 1 == len(steps)
        if rank == 0:
            seed_rows, seeds = kernel_call(
                seeds_kernel, "seeds", [seed_mask.reshape(chunks, LANES), profiles, row_sum], (f32_rows, bf16_rows), 1
            )
            peer_seeds = [to_peer(seeds, step) for step in range(min(2, len(steps)))]
        ins = [pack, peer_packs[step], hl, row_sum, col_sum]
        degrees = jax.ShapeDtypeStruct((2 * chunks, LANES), F32)
        out = kernel_call(
            lambda *refs, offsets=offsets, last=last: peer_weights_kernel((blocks, last), offsets, *refs),
            "peer_weights",
            ins,
            (weights_of(blocks * blocks), degrees) if last else (weights_of(blocks * blocks), f32_rows, f32_rows),
            blocks * blocks * tile_flops,
            [pltpu.VMEM((mols, LANES), F32)] * 2 + [one_tile] if last else [one_tile],
        )
        weights[1 + step] = out[0]
        if last:
            degree = out[1]
        else:
            row_sum, col_sum = out[1:]
        if rank == 0:
            held_seeds, row_sum = lax.optimization_barrier((peer_seeds[0], row_sum))
            peer_seeds.append(lax.ppermute(held_seeds, ("row", "col"), list(steps[2][0].items())))
    scales = kernel_call(degree_kernel, "degree", [degree, other_core(degree)], degrees, 1)
    peer_scales = [to_peer(scales, step) for step in range(len(steps) - 1)]
    held_scales, peer_seeds[0] = lax.optimization_barrier((scales, peer_seeds[0]))
    peer_scales.append(to_peer(held_scales, len(steps) - 1))
    own_scales, peer_seeds[1] = lax.optimization_barrier((scales, peer_seeds[1]))
    scaled, row_scale, col_scale = kernel_call(
        expand_kernel, "expand", [own_scales, seed_rows], (bf16_rows, f32_rows, f32_rows), 1
    )
    for iteration in range(ITERS):
        first = iteration == 0
        peers = peer_seeds if first else from_peers(scaled, FORWARD[2])
        partial = kernel_call(
            lambda *refs: product_kernel(blocks, None, False, *refs),
            "own_product",
            [pack, weights[0], scaled],
            f32_rows,
            blocks * tile_flops,
        )
        if not first:
            held, partial = lax.optimization_barrier((scaled, partial))
            peers[1] = to_peer(held, 1)
        for step in [1, 0, 2]:
            offsets = steps[step][1]
            final = step + 1 == len(steps)
            partial = kernel_call(
                lambda *refs, offsets=offsets, first=first: product_kernel(blocks, offsets, first, *refs),
                "peer_product",
                [pack, weights[1 + step], peers[step]] + [peer_scales[step]] * first + [partial],
                bf16_rows if final else f32_rows,
                blocks * blocks * tile_flops,
                [pltpu.VMEM((mols, LANES), BF16)] * first,
            )
        other = other_core(partial)
        if iteration + 1 < ITERS:
            scaled = kernel_call(
                state_kernel, "state", [partial, other, row_scale, seed_rows, col_scale], bf16_rows, 1
            )
    return (partial.astype(F32) + other.astype(F32)) * row_scale + (1.0 - ALPHA) * seed_rows


def solution(mesh):
    placed = (
        P(("grp", "row"), None),
        P(("grp", "row"), None),
        P(("grp", "row")),
        P(("grp", "row"), None),
        P(("grp", "row")),
    )
    return jax.shard_map(
        shards, mesh=mesh, in_specs=placed, out_specs=P(("grp", "row"), None), check_vma=False
    )
```

```python
import jax
import jax.numpy as jnp
from jax import lax
from jax.experimental import pallas as pl
from jax.experimental.pallas import tpu as pltpu
from jax.sharding import PartitionSpec as P

BAND = 6
ITERS = 2

KERNEL_SCALE = 12.5
ALPHA = 0.8
EPS = 1e-06
LOG2E = 1.4426950408889634
LANES = 128
TAIL = 16
F32 = jnp.float32
BF16 = jnp.bfloat16

VMEM = pl.BlockSpec(memory_space=pltpu.VMEM)
HBM = pl.BlockSpec(memory_space=pltpu.HBM)
PARAMS = pltpu.CompilerParams(vmem_limit_bytes=24 * 1024 * 1024)


FORWARD = (True, True, True)


def distance_of(chip, device, cols):
    return abs(chip - device // cols)


def complete(moves, rows, cols, fixed):
    moves = dict(moves)
    sources = [n for n in range(rows * cols) if n not in moves]
    targets = [n for n in range(rows * cols) if n not in moves.values()]
    for s in list(sources):
        other = [t for t in targets if t // cols == s // cols and t != s]
        if other:
            moves[s] = other[0]
            sources.remove(s)
            targets.remove(other[0])
    for s in list(sources):
        if s in targets:
            y = s ^ 1
            if fixed:
                moves[s] = moves[y]
                moves[y] = s
            else:
                z = next(n for n, t in moves.items() if t == y)
                moves[z] = s
                moves[s] = y
            sources.remove(s)
            targets.remove(s)
    for s, t in zip(sources, targets):
        moves[s] = t
    return moves


def landings(moves, origin, rows, cols, distance):
    table = [[0] * rows for _ in range(cols)]
    for s, t in moves.items():
        if origin(s) is not None and distance_of(origin(s), t, cols) == distance:
            table[t % cols][t // cols] = origin(s) - t // cols
    return table


def exchange_steps(rows, cols, reach):
    steps = []
    for d in range(1, reach + 1):
        if d < 3:
            moves = {}
            for a in range(rows - d):
                core = a // d % cols
                moves[a * cols + core] = (a + d) * cols + core
                moves[(a + d) * cols + core] = a * cols + core
            moves = complete(moves, rows, cols, False)
            table = landings(moves, lambda s: s // cols, rows, cols, d)
            steps.append((moves, table, moves))
            continue
        held = steps[d - 3][1]

        def origin(s, held=held):
            offset = held[s % cols][s // cols]
            return s // cols + offset if offset else None

        moves, taken = {}, [0] * rows
        for s in range(rows * cols):
            if origin(s) is not None:
                t = s // cols + (2 if origin(s) < s // cols else -2)
                if 0 <= t < rows:
                    moves[s] = t * cols + taken[t]
                    taken[t] += 1
        moves = complete(moves, rows, cols, False)
        table = landings(moves, origin, rows, cols, d)
        direct, sent = {}, [0] * rows
        for chip in range(rows):
            for core in range(cols):
                if table[core][chip]:
                    source = chip + table[core][chip]
                    direct[source * cols + sent[source]] = chip * cols + core
                    sent[source] += 1
        direct = complete(direct, rows, cols, True)
        steps.append((moves, table, direct))
    return steps


def peer_offset(offsets):
    r, c = lax.axis_index("row"), lax.axis_index("col")
    value = jnp.int32(0)
    for core, per_row in enumerate(offsets):
        for word, first in enumerate(range(0, len(per_row), 8)):
            code = sum((offset + 8) << (4 * n) for n, offset in enumerate(per_row[first : first + 8]))
            code = jnp.int32(code - (1 << 32) if code >= 1 << 31 else code)
            digit = (lax.shift_right_logical(code, 4 * lax.rem(r, 8)) & 15) - 8
            here = jnp.logical_and(c == core, lax.div(r, 8) == word)
            value = jnp.where(here, digit, value)
    return value


def table_entry(table, row, offset):
    lane = lax.broadcasted_iota(jnp.int32, (1, LANES), 1)
    return jnp.max(jnp.where(lane == offset + BAND, table[row : row + 1, :], 0.0), axis=-1, keepdims=True)


def lanes_sum(w):
    part = w[:, :LANES]
    for k in range(1, w.shape[1] // LANES):
        part = part + w[:, k * LANES : (k + 1) * LANES]
    return part


def pack_kernel(blocks, slots, emb_hbm, cols_hbm, count_hbm, out_ref, cols_ref, count_ref, sems):
    mols = emb_hbm.shape[0]
    loads = [
        pltpu.make_async_copy(emb_hbm, out_ref.at[pl.ds(0, mols), :], sems.at[0]),
        pltpu.make_async_copy(cols_hbm, cols_ref, sems.at[1]),
        pltpu.make_async_copy(count_hbm, count_ref, sems.at[2]),
    ]
    for load in loads:
        load.start()
    loads[1].wait()
    loads[2].wait()
    first = lax.axis_index("row") * blocks
    lane = lax.broadcasted_iota(jnp.int32, (TAIL, LANES), 1)
    row = lax.broadcasted_iota(jnp.int32, (TAIL, LANES), 0)
    table = jnp.zeros((TAIL, LANES), F32)
    for b in range(blocks):
        for s in range(slots):
            offset = jnp.where(s < count_ref[b], cols_ref[b, s] - (first + b) + BAND, -1)
            table = jnp.where(jnp.logical_and(lane == offset, row == b), 1.0, table)
    out_ref[pl.ds(mols, TAIL), :] = table.astype(BF16)
    loads[0].wait()


def compact(column):
    eye = lax.broadcasted_iota(jnp.int32, (LANES, LANES), 0) == lax.broadcasted_iota(jnp.int32, (LANES, LANES), 1)
    rows = []
    for k in range(column.shape[0] // LANES):
        rows.append(jnp.sum(jnp.where(eye, column[k * LANES : (k + 1) * LANES], 0.0), axis=0, keepdims=True))
    return jnp.concatenate(rows, axis=0)


def tile_weights(hl, b, e, w_ref, at, s_ref, diagonal):
    size, width = e.shape
    x = e.astype(F32)
    x = x * x
    high = x.astype(BF16)
    both = jnp.concatenate([high, (x - high.astype(F32)).astype(BF16)], axis=1)
    nt = (((1,), (1,)), ((), ()))
    total = lax.dot_general(jnp.ones((TAIL, 2 * width), BF16), both, nt, preferred_element_type=F32)
    inv = lax.rsqrt(total[0:1] * (1.0 / width) + EPS)
    ee = jnp.concatenate([e, e], axis=1)
    s_ref[...] = lax.dot_general(hl[pl.ds(b * size, size), :], ee, nt, preferred_element_type=F32)
    parts = []
    rows = 32
    for k in range(size // rows):
        w = jnp.exp2(s_ref[pl.ds(k * rows, rows), :] * inv - 2.0 * KERNEL_SCALE * LOG2E)
        if diagonal is not None:
            i = lax.broadcasted_iota(jnp.int32, (rows, size), 0) + k * rows
            j = lax.broadcasted_iota(jnp.int32, (rows, size), 1)
            w = jnp.where(jnp.logical_and(i == j, diagonal), 0.0, w)
        w_ref[at, pl.ds(k * rows, rows), :] = w.astype(BF16)
        parts.append(lanes_sum(w))
    return parts


def add_parts(ref, first, parts, mask, start):
    rows = parts[0].shape[0]
    for k, part in enumerate(parts):
        at = pl.ds(first + k * rows, rows)
        value = part * mask
        ref[at, :] = value if start else ref[at, :] + value


def own_weights_kernel(blocks, pack_ref, hl, w_ref, row_ref, col_ref, s_ref):
    mols = hl.shape[0]
    size, width = mols // blocks, hl.shape[1] // 2
    c = lax.axis_index("col")
    table = pack_ref[pl.ds(mols, TAIL), :].astype(F32)
    for b in range(blocks):
        x = pack_ref[pl.ds(b * size, size), :].astype(F32)
        scale = lax.rsqrt(jnp.sum(x * x, axis=-1, keepdims=True) * (1.0 / width) + EPS)
        x = x * (scale * (2.0 * KERNEL_SCALE * LOG2E / width))
        high = x.astype(BF16)
        hl[pl.ds(b * size, size), :width] = high
        hl[pl.ds(b * size, size), width:] = (x - high.astype(F32)).astype(BF16)
    e = pack_ref[pl.ds(pl.multiple_of(c * size, size), size), :]
    for b in range(blocks):
        parts = tile_weights(hl, b, e, w_ref, b, s_ref, c == b)
        from_c = jnp.where(c == 0, table_entry(table, 0, b), table_entry(table, 1, b - 1))
        add_parts(row_ref, b * size, parts, table_entry(table, b, c - b), True)
        add_parts(col_ref, b * size, parts, from_c, True)


def peer_weights_kernel(dims, offsets, pack_ref, peer_ref, hl, row_in, col_in, w_ref, *rest):
    blocks, last = dims
    if last:
        deg_ref, row_ref, col_ref, s_ref = rest
    else:
        row_ref, col_ref, s_ref = rest
    mols = hl.shape[0]
    size = mols // blocks
    chips = peer_offset(offsets)
    valid = jnp.where(chips != 0, 1.0, 0.0)
    own_table = pack_ref[pl.ds(mols, TAIL), :].astype(F32) * valid
    peer_table = peer_ref[pl.ds(mols, TAIL), :].astype(F32) * valid
    row_ref[...] = row_in[...]
    col_ref[...] = col_in[...]
    for k in range(blocks):
        e = peer_ref[pl.ds(k * size, size), :]
        for b in range(blocks):
            offset = chips * blocks + (k - b)
            parts = tile_weights(hl, b, e, w_ref, k * blocks + b, s_ref, None)
            add_parts(row_ref, b * size, parts, table_entry(own_table, b, offset), False)
            add_parts(col_ref, b * size, parts, table_entry(peer_table, k, -offset), False)
    if last:
        half = mols // LANES
        for n, ref in enumerate((row_ref, col_ref)):
            deg_ref[pl.ds(n * half, half), :] = compact(jnp.sum(ref[...], axis=-1, keepdims=True))


def seeds_kernel(mask_ref, profile_ref, after_ref, seed_ref, bf16_ref):
    del after_ref
    columns = mask_ref[...].astype(F32).T
    for k in range(mask_ref.shape[0]):
        at = pl.ds(k * LANES, LANES)
        seed = jnp.where(columns[:, k : k + 1] > 0.0, profile_ref[at, :], 0.0)
        seed_ref[at, :] = seed
        bf16_ref[at, :] = seed.astype(BF16)


def degree_kernel(own_ref, other_ref, out_ref):
    out_ref[...] = lax.rsqrt(own_ref[...] + other_ref[...])


def expand_kernel(scales_ref, seed_ref, scaled_ref, rs_ref, cs_ref):
    columns = scales_ref[...].T
    half = scales_ref.shape[0] // 2
    for k in range(half):
        at = pl.ds(k * LANES, LANES)
        by_col = jnp.broadcast_to(columns[:, half + k : half + k + 1], (LANES, LANES))
        rs_ref[at, :] = jnp.broadcast_to(columns[:, k : k + 1] * ALPHA, (LANES, LANES))
        cs_ref[at, :] = by_col
        scaled_ref[at, :] = (seed_ref[at, :] * by_col).astype(BF16)


def product_kernel(blocks, offsets, first, pack_ref, w_ref, scaled_ref, *rest):
    if first:
        scales_ref, _, out_ref, product_ref = rest
        columns = scales_ref[...].T
        half = scales_ref.shape[0] // 2
        for k in range(half):
            at = pl.ds(k * LANES, LANES)
            seed = scaled_ref[at, :].astype(F32)
            product_ref[at, :] = (seed * columns[:, half + k : half + k + 1]).astype(BF16)
        scaled_ref, rest = product_ref, rest[1:]
    else:
        out_ref = rest[-1]
    mols = scaled_ref.shape[0]
    size = mols // blocks
    table = pack_ref[pl.ds(mols, TAIL), :].astype(F32)
    c = lax.axis_index("col")
    if offsets is not None:
        chips = peer_offset(offsets)
        table = table * jnp.where(chips != 0, 1.0, 0.0)
    for b in range(blocks):
        at = pl.ds(b * size, size)
        if offsets is None:
            s = scaled_ref[pl.ds(pl.multiple_of(c * size, size), size), :].astype(F32)
            s = (s * table_entry(table, b, c - b)).astype(BF16)
            out_ref[at, :] = jnp.dot(w_ref[b], s, preferred_element_type=F32)
            continue
        total = rest[0][at, :]
        for k in range(blocks):
            offset = chips * blocks + (k - b)
            s = scaled_ref[pl.ds(k * size, size), :].astype(F32)
            s = (s * table_entry(table, b, offset)).astype(BF16)
            total = total + jnp.dot(w_ref[k * blocks + b], s, preferred_element_type=F32)
        out_ref[at, :] = total.astype(out_ref.dtype)


def state_kernel(own_ref, other_ref, rs_ref, seed_ref, cs_ref, out_ref):
    state = (own_ref[...].astype(F32) + other_ref[...].astype(F32)) * rs_ref[...] + (1.0 - ALPHA) * seed_ref[...]
    out_ref[...] = (state * cs_ref[...]).astype(BF16)


def spread_kernel(own_ref, other_ref, rs_ref, seed_ref, out_hbm, out_ref, sems):
    chunks = sems.shape[0]
    size = out_ref.shape[0] // chunks
    copies = []
    for n in range(chunks):
        at = pl.ds(n * size, size)
        total = own_ref[at, :].astype(F32) + other_ref[at, :].astype(F32)
        out_ref[at, :] = total * rs_ref[at, :] + (1.0 - ALPHA) * seed_ref[at, :]
        copies.append(pltpu.make_async_copy(out_ref.at[at, :], out_hbm.at[at, :], sems.at[n]))
        copies[-1].start()
    for copy in copies:
        copy.wait()


def kernel_call(body, name, ins, outs, flops, scratch=(), in_specs=None, out_specs=None):
    return pl.pallas_call(
        body,
        out_shape=outs,
        in_specs=in_specs or [VMEM] * len(ins),
        out_specs=out_specs or jax.tree.map(lambda _: VMEM, outs),
        scratch_shapes=scratch,
        compiler_params=PARAMS,
        cost_estimate=pl.CostEstimate(flops=flops, bytes_accessed=1 << 20, transcendentals=0),
        name=name,
    )(*ins)


def shards(embeddings, profiles, seed_mask, tile_cols, tile_count):
    rows, cols = lax.axis_size("row"), lax.axis_size("col")
    blocks, slots = tile_cols.shape
    mols, width = embeddings.shape
    prof = profiles.shape[1]
    size = mols // blocks
    reach = (BAND + blocks - 1) // blocks
    assert blocks == 2 and cols == 2 and width == LANES and prof == LANES
    steps = exchange_steps(rows, cols, reach)
    f32_rows = jax.ShapeDtypeStruct((mols, LANES), F32)
    bf16_rows = jax.ShapeDtypeStruct((mols, LANES), BF16)
    tile_flops = 4 * size * size * width

    def to_peer(value, step):
        return lax.ppermute(value, ("row", "col"), list(steps[step][2].items()))

    def from_peers(value, forward=False):
        pieces = []
        for step, (moves, _, _) in enumerate(steps):
            if forward and step > 1:
                pieces.append(lax.ppermute(pieces[step - 2], ("row", "col"), list(moves.items())))
            else:
                pieces.append(to_peer(value, step))
        return pieces

    def other_core(value):
        return lax.ppermute(value, "col", [(0, 1), (1, 0)])

    def weights_of(tiles):
        return jax.ShapeDtypeStruct((tiles, size, size), BF16)

    chunks = mols // LANES
    held = [pltpu.with_memory_space_constraint(t, pltpu.HBM) for t in (embeddings, tile_cols, tile_count)]
    pack = kernel_call(
        lambda *refs: pack_kernel(blocks, slots, *refs),
        "pack",
        held,
        jax.ShapeDtypeStruct((mols + TAIL, LANES), BF16),
        1,
        [
            pltpu.SMEM(tile_cols.shape, jnp.int32),
            pltpu.SMEM(tile_count.shape, jnp.int32),
            pltpu.SemaphoreType.DMA((3,)),
        ],
        [HBM] * 3,
    )
    peer_packs = from_peers(pack, FORWARD[0])
    one_tile = pltpu.VMEM((size, size), F32)
    hl, own_weights, row_sum, col_sum = kernel_call(
        lambda *refs: own_weights_kernel(blocks, *refs),
        "own_weights",
        [pack],
        (jax.ShapeDtypeStruct((mols, 2 * width), BF16), weights_of(blocks), f32_rows, f32_rows),
        blocks * tile_flops,
        [one_tile],
    )
    weights = [own_weights] + [None] * len(steps)
    for rank, step in enumerate([1, 0, 2]):
        offsets = steps[step][1]
        last = rank + 1 == len(steps)
        if rank == 0:
            seed_rows, seeds = kernel_call(
                seeds_kernel, "seeds", [seed_mask.reshape(chunks, LANES), profiles, row_sum], (f32_rows, bf16_rows), 1
            )
            peer_seeds = [to_peer(seeds, step) for step in range(min(2, len(steps)))]
        ins = [pack, peer_packs[step], hl, row_sum, col_sum]
        degrees = jax.ShapeDtypeStruct((2 * chunks, LANES), F32)
        out = kernel_call(
            lambda *refs, offsets=offsets, last=last: peer_weights_kernel((blocks, last), offsets, *refs),
            "peer_weights",
            ins,
            (weights_of(blocks * blocks), degrees) if last else (weights_of(blocks * blocks), f32_rows, f32_rows),
            blocks * blocks * tile_flops,
            [pltpu.VMEM((mols, LANES), F32)] * 2 + [one_tile] if last else [one_tile],
        )
        weights[1 + step] = out[0]
        if last:
            degree = out[1]
        else:
            row_sum, col_sum = out[1:]
        if rank == 0:
            held_seeds, row_sum = lax.optimization_barrier((peer_seeds[0], row_sum))
            peer_seeds.append(lax.ppermute(held_seeds, ("row", "col"), list(steps[2][0].items())))
    scales = kernel_call(degree_kernel, "degree", [degree, other_core(degree)], degrees, 1)
    peer_scales = [to_peer(scales, step) for step in range(len(steps) - 1)]
    held_scales, peer_seeds[0] = lax.optimization_barrier((scales, peer_seeds[0]))
    peer_scales.append(to_peer(held_scales, len(steps) - 1))
    own_scales, peer_seeds[1] = lax.optimization_barrier((scales, peer_seeds[1]))
    scaled, row_scale, col_scale = kernel_call(
        expand_kernel, "expand", [own_scales, seed_rows], (bf16_rows, f32_rows, f32_rows), 1
    )
    for iteration in range(ITERS):
        first = iteration == 0
        peers = peer_seeds if first else from_peers(scaled, FORWARD[2])
        partial = kernel_call(
            lambda *refs: product_kernel(blocks, None, False, *refs),
            "own_product",
            [pack, weights[0], scaled],
            f32_rows,
            blocks * tile_flops,
        )
        if not first:
            held, partial = lax.optimization_barrier((scaled, partial))
            peers[1] = to_peer(held, 1)
        for step in [1, 0, 2]:
            offsets = steps[step][1]
            final = step + 1 == len(steps)
            partial = kernel_call(
                lambda *refs, offsets=offsets, first=first: product_kernel(blocks, offsets, first, *refs),
                "peer_product",
                [pack, weights[1 + step], peers[step]] + [peer_scales[step]] * first + [partial],
                bf16_rows if final else f32_rows,
                blocks * blocks * tile_flops,
                [pltpu.VMEM((mols, LANES), BF16)] * first,
            )
        other = other_core(partial)
        if iteration + 1 < ITERS:
            scaled = kernel_call(
                state_kernel, "state", [partial, other, row_scale, seed_rows, col_scale], bf16_rows, 1
            )
    return kernel_call(
        spread_kernel,
        "spread",
        [partial, other, row_scale, seed_rows],
        pltpu.HBM((mols, LANES), F32),
        1,
        [pltpu.VMEM((mols, LANES), F32), pltpu.SemaphoreType.DMA((4,))],
        out_specs=HBM,
    )


def solution(mesh):
    placed = (
        P(("grp", "row"), None),
        P(("grp", "row"), None),
        P(("grp", "row")),
        P(("grp", "row"), None),
        P(("grp", "row")),
    )
    return jax.shard_map(
        shards, mesh=mesh, in_specs=placed, out_specs=P(("grp", "row"), None), check_vma=False
    )
```

```python
import jax
import jax.numpy as jnp
from jax import lax
from jax.experimental import pallas as pl
from jax.experimental.pallas import tpu as pltpu
from jax.sharding import PartitionSpec as P

BAND = 6
ITERS = 2

KERNEL_SCALE = 12.5
ALPHA = 0.8
EPS = 1e-06
LOG2E = 1.4426950408889634
LANES = 128
TAIL = 16
F32 = jnp.float32
BF16 = jnp.bfloat16

VMEM = pl.BlockSpec(memory_space=pltpu.VMEM)
HBM = pl.BlockSpec(memory_space=pltpu.HBM)
PARAMS = pltpu.CompilerParams(vmem_limit_bytes=24 * 1024 * 1024)


FORWARD = (True, True, True)


def distance_of(chip, device, cols):
    return abs(chip - device // cols)


def complete(moves, rows, cols, fixed):
    moves = dict(moves)
    sources = [n for n in range(rows * cols) if n not in moves]
    targets = [n for n in range(rows * cols) if n not in moves.values()]
    for s in list(sources):
        other = [t for t in targets if t // cols == s // cols and t != s]
        if other:
            moves[s] = other[0]
            sources.remove(s)
            targets.remove(other[0])
    for s in list(sources):
        if s in targets:
            y = s ^ 1
            if fixed:
                moves[s] = moves[y]
                moves[y] = s
            else:
                z = next(n for n, t in moves.items() if t == y)
                moves[z] = s
                moves[s] = y
            sources.remove(s)
            targets.remove(s)
    for s, t in zip(sources, targets):
        moves[s] = t
    return moves


def landings(moves, origin, rows, cols, distance):
    table = [[0] * rows for _ in range(cols)]
    for s, t in moves.items():
        if origin(s) is not None and distance_of(origin(s), t, cols) == distance:
            table[t % cols][t // cols] = origin(s) - t // cols
    return table


def exchange_steps(rows, cols, reach):
    steps = []
    for d in range(1, reach + 1):
        if d < 3:
            moves = {}
            for a in range(rows - d):
                core = a // d % cols
                moves[a * cols + core] = (a + d) * cols + core
                moves[(a + d) * cols + core] = a * cols + core
            moves = complete(moves, rows, cols, False)
            table = landings(moves, lambda s: s // cols, rows, cols, d)
            steps.append((moves, table, moves))
            continue
        held = steps[d - 3][1]

        def origin(s, held=held):
            offset = held[s % cols][s // cols]
            return s // cols + offset if offset else None

        moves, taken = {}, [0] * rows
        for s in range(rows * cols):
            if origin(s) is not None:
                t = s // cols + (2 if origin(s) < s // cols else -2)
                if 0 <= t < rows:
                    moves[s] = t * cols + taken[t]
                    taken[t] += 1
        moves = complete(moves, rows, cols, False)
        table = landings(moves, origin, rows, cols, d)
        direct, sent = {}, [0] * rows
        for chip in range(rows):
            for core in range(cols):
                if table[core][chip]:
                    source = chip + table[core][chip]
                    direct[source * cols + sent[source]] = chip * cols + core
                    sent[source] += 1
        direct = complete(direct, rows, cols, True)
        steps.append((moves, table, direct))
    return steps


def peer_offset(offsets):
    r, c = lax.axis_index("row"), lax.axis_index("col")
    value = jnp.int32(0)
    for core, per_row in enumerate(offsets):
        for word, first in enumerate(range(0, len(per_row), 8)):
            code = sum((offset + 8) << (4 * n) for n, offset in enumerate(per_row[first : first + 8]))
            code = jnp.int32(code - (1 << 32) if code >= 1 << 31 else code)
            digit = (lax.shift_right_logical(code, 4 * lax.rem(r, 8)) & 15) - 8
            here = jnp.logical_and(c == core, lax.div(r, 8) == word)
            value = jnp.where(here, digit, value)
    return value


def table_entry(table, row, offset):
    lane = lax.broadcasted_iota(jnp.int32, (1, LANES), 1)
    return jnp.max(jnp.where(lane == offset + BAND, table[row : row + 1, :], 0.0), axis=-1, keepdims=True)


def lanes_sum(w):
    part = w[:, :LANES]
    for k in range(1, w.shape[1] // LANES):
        part = part + w[:, k * LANES : (k + 1) * LANES]
    return part


def pack_kernel(blocks, slots, emb_hbm, cols_hbm, count_hbm, out_ref, cols_ref, count_ref, sems):
    mols = emb_hbm.shape[0]
    loads = [
        pltpu.make_async_copy(emb_hbm, out_ref.at[pl.ds(0, mols), :], sems.at[0]),
        pltpu.make_async_copy(cols_hbm, cols_ref, sems.at[1]),
        pltpu.make_async_copy(count_hbm, count_ref, sems.at[2]),
    ]
    for load in loads:
        load.start()
    loads[1].wait()
    loads[2].wait()
    first = lax.axis_index("row") * blocks
    lane = lax.broadcasted_iota(jnp.int32, (TAIL, LANES), 1)
    row = lax.broadcasted_iota(jnp.int32, (TAIL, LANES), 0)
    table = jnp.zeros((TAIL, LANES), F32)
    for b in range(blocks):
        for s in range(slots):
            offset = jnp.where(s < count_ref[b], cols_ref[b, s] - (first + b) + BAND, -1)
            table = jnp.where(jnp.logical_and(lane == offset, row == b), 1.0, table)
    out_ref[pl.ds(mols, TAIL), :] = table.astype(BF16)
    loads[0].wait()


def compact(column):
    eye = lax.broadcasted_iota(jnp.int32, (LANES, LANES), 0) == lax.broadcasted_iota(jnp.int32, (LANES, LANES), 1)
    rows = []
    for k in range(column.shape[0] // LANES):
        rows.append(jnp.sum(jnp.where(eye, column[k * LANES : (k + 1) * LANES], 0.0), axis=0, keepdims=True))
    return jnp.concatenate(rows, axis=0)


def tile_weights(hl, b, e, w_ref, at, s_ref, diagonal):
    size, width = e.shape
    x = e.astype(F32)
    x = x * x
    high = x.astype(BF16)
    both = jnp.concatenate([high, (x - high.astype(F32)).astype(BF16)], axis=1)
    nt = (((1,), (1,)), ((), ()))
    total = lax.dot_general(jnp.ones((TAIL, 2 * width), BF16), both, nt, preferred_element_type=F32)
    inv = lax.rsqrt(total[0:1] * (1.0 / width) + EPS)
    ee = jnp.concatenate([e, e], axis=1)
    s_ref[...] = lax.dot_general(hl[pl.ds(b * size, size), :], ee, nt, preferred_element_type=F32)
    parts = []
    rows = 32
    for k in range(size // rows):
        w = jnp.exp2(s_ref[pl.ds(k * rows, rows), :] * inv - 2.0 * KERNEL_SCALE * LOG2E)
        if diagonal is not None:
            i = lax.broadcasted_iota(jnp.int32, (rows, size), 0) + k * rows
            j = lax.broadcasted_iota(jnp.int32, (rows, size), 1)
            w = jnp.where(jnp.logical_and(i == j, diagonal), 0.0, w)
        w_ref[at, pl.ds(k * rows, rows), :] = w.astype(BF16)
        parts.append(lanes_sum(w))
    return parts


def add_parts(ref, first, parts, mask, source):
    rows = parts[0].shape[0]
    for k, part in enumerate(parts):
        at = pl.ds(first + k * rows, rows)
        value = part * mask
        ref[at, :] = value if source is None else source[at, :] + value


def own_weights_kernel(blocks, pack_ref, hl, w_ref, row_ref, col_ref, s_ref):
    mols = hl.shape[0]
    size, width = mols // blocks, hl.shape[1] // 2
    c = lax.axis_index("col")
    table = pack_ref[pl.ds(mols, TAIL), :].astype(F32)
    for b in range(blocks):
        x = pack_ref[pl.ds(b * size, size), :].astype(F32)
        scale = lax.rsqrt(jnp.sum(x * x, axis=-1, keepdims=True) * (1.0 / width) + EPS)
        x = x * (scale * (2.0 * KERNEL_SCALE * LOG2E / width))
        high = x.astype(BF16)
        hl[pl.ds(b * size, size), :width] = high
        hl[pl.ds(b * size, size), width:] = (x - high.astype(F32)).astype(BF16)
    e = pack_ref[pl.ds(pl.multiple_of(c * size, size), size), :]
    for b in range(blocks):
        parts = tile_weights(hl, b, e, w_ref, b, s_ref, c == b)
        from_c = jnp.where(c == 0, table_entry(table, 0, b), table_entry(table, 1, b - 1))
        add_parts(row_ref, b * size, parts, table_entry(table, b, c - b), None)
        add_parts(col_ref, b * size, parts, from_c, None)


def peer_weights_kernel(dims, offsets, pack_ref, peer_ref, hl, row_in, col_in, w_ref, *rest):
    blocks, last = dims
    if last:
        deg_ref, row_ref, col_ref, s_ref = rest
    else:
        row_ref, col_ref, s_ref = rest
    mols = hl.shape[0]
    size = mols // blocks
    chips = peer_offset(offsets)
    valid = jnp.where(chips != 0, 1.0, 0.0)
    own_table = pack_ref[pl.ds(mols, TAIL), :].astype(F32) * valid
    peer_table = peer_ref[pl.ds(mols, TAIL), :].astype(F32) * valid
    for k in range(blocks):
        e = peer_ref[pl.ds(k * size, size), :]
        for b in range(blocks):
            offset = chips * blocks + (k - b)
            parts = tile_weights(hl, b, e, w_ref, k * blocks + b, s_ref, None)
            add_parts(row_ref, b * size, parts, table_entry(own_table, b, offset), row_in if k == 0 else row_ref)
            add_parts(col_ref, b * size, parts, table_entry(peer_table, k, -offset), col_in if k == 0 else col_ref)
    if last:
        half = mols // LANES
        for n, ref in enumerate((row_ref, col_ref)):
            deg_ref[pl.ds(n * half, half), :] = compact(jnp.sum(ref[...], axis=-1, keepdims=True))


def seeds_kernel(mask_ref, profile_ref, after_ref, seed_ref, bf16_ref):
    del after_ref
    columns = mask_ref[...].astype(F32).T
    for k in range(mask_ref.shape[0]):
        at = pl.ds(k * LANES, LANES)
        seed = jnp.where(columns[:, k : k + 1] > 0.0, profile_ref[at, :], 0.0)
        seed_ref[at, :] = seed
        bf16_ref[at, :] = seed.astype(BF16)


def degree_kernel(own_ref, other_ref, out_ref):
    out_ref[...] = lax.rsqrt(own_ref[...] + other_ref[...])


def expand_kernel(scales_ref, seed_ref, scaled_ref, rs_ref, cs_ref):
    columns = scales_ref[...].T
    half = scales_ref.shape[0] // 2
    for k in range(half):
        at = pl.ds(k * LANES, LANES)
        by_col = jnp.broadcast_to(columns[:, half + k : half + k + 1], (LANES, LANES))
        rs_ref[at, :] = jnp.broadcast_to(columns[:, k : k + 1] * ALPHA, (LANES, LANES))
        cs_ref[at, :] = by_col
        scaled_ref[at, :] = (seed_ref[at, :] * by_col).astype(BF16)


def product_kernel(blocks, offsets, first, pack_ref, w_ref, scaled_ref, *rest):
    if first:
        scales_ref, _, out_ref, product_ref = rest
        columns = scales_ref[...].T
        half = scales_ref.shape[0] // 2
        for k in range(half):
            at = pl.ds(k * LANES, LANES)
            seed = scaled_ref[at, :].astype(F32)
            product_ref[at, :] = (seed * columns[:, half + k : half + k + 1]).astype(BF16)
        scaled_ref, rest = product_ref, rest[1:]
    else:
        out_ref = rest[-1]
    mols = scaled_ref.shape[0]
    size = mols // blocks
    table = pack_ref[pl.ds(mols, TAIL), :].astype(F32)
    c = lax.axis_index("col")
    if offsets is not None:
        chips = peer_offset(offsets)
        table = table * jnp.where(chips != 0, 1.0, 0.0)
    for b in range(blocks):
        at = pl.ds(b * size, size)
        if offsets is None:
            s = scaled_ref[pl.ds(pl.multiple_of(c * size, size), size), :].astype(F32)
            s = (s * table_entry(table, b, c - b)).astype(BF16)
            out_ref[at, :] = jnp.dot(w_ref[b], s, preferred_element_type=F32)
            continue
        total = rest[0][at, :]
        for k in range(blocks):
            offset = chips * blocks + (k - b)
            s = scaled_ref[pl.ds(k * size, size), :].astype(F32)
            s = (s * table_entry(table, b, offset)).astype(BF16)
            total = total + jnp.dot(w_ref[k * blocks + b], s, preferred_element_type=F32)
        out_ref[at, :] = total.astype(out_ref.dtype)


def state_kernel(own_ref, other_ref, rs_ref, seed_ref, cs_ref, out_ref):
    state = (own_ref[...].astype(F32) + other_ref[...].astype(F32)) * rs_ref[...] + (1.0 - ALPHA) * seed_ref[...]
    out_ref[...] = (state * cs_ref[...]).astype(BF16)


def kernel_call(body, name, ins, outs, flops, scratch=(), in_specs=None):
    return pl.pallas_call(
        body,
        out_shape=outs,
        in_specs=in_specs or [VMEM] * len(ins),
        out_specs=jax.tree.map(lambda _: VMEM, outs),
        scratch_shapes=scratch,
        compiler_params=PARAMS,
        cost_estimate=pl.CostEstimate(flops=flops, bytes_accessed=1 << 20, transcendentals=0),
        name=name,
    )(*ins)


def shards(embeddings, profiles, seed_mask, tile_cols, tile_count):
    rows, cols = lax.axis_size("row"), lax.axis_size("col")
    blocks, slots = tile_cols.shape
    mols, width = embeddings.shape
    prof = profiles.shape[1]
    size = mols // blocks
    reach = (BAND + blocks - 1) // blocks
    assert blocks == 2 and cols == 2 and width == LANES and prof == LANES
    steps = exchange_steps(rows, cols, reach)
    f32_rows = jax.ShapeDtypeStruct((mols, LANES), F32)
    bf16_rows = jax.ShapeDtypeStruct((mols, LANES), BF16)
    tile_flops = 4 * size * size * width

    def to_peer(value, step):
        return lax.ppermute(value, ("row", "col"), list(steps[step][2].items()))

    def from_peers(value, forward=False):
        pieces = []
        for step, (moves, _, _) in enumerate(steps):
            if forward and step > 1:
                pieces.append(lax.ppermute(pieces[step - 2], ("row", "col"), list(moves.items())))
            else:
                pieces.append(to_peer(value, step))
        return pieces

    def other_core(value):
        return lax.ppermute(value, "col", [(0, 1), (1, 0)])

    def weights_of(tiles):
        return jax.ShapeDtypeStruct((tiles, size, size), BF16)

    chunks = mols // LANES
    held = [pltpu.with_memory_space_constraint(t, pltpu.HBM) for t in (embeddings, tile_cols, tile_count)]
    pack = kernel_call(
        lambda *refs: pack_kernel(blocks, slots, *refs),
        "pack",
        held,
        jax.ShapeDtypeStruct((mols + TAIL, LANES), BF16),
        1,
        [
            pltpu.SMEM(tile_cols.shape, jnp.int32),
            pltpu.SMEM(tile_count.shape, jnp.int32),
            pltpu.SemaphoreType.DMA((3,)),
        ],
        [HBM] * 3,
    )
    peer_packs = from_peers(pack, FORWARD[0])
    one_tile = pltpu.VMEM((size, size), F32)
    hl, own_weights, row_sum, col_sum = kernel_call(
        lambda *refs: own_weights_kernel(blocks, *refs),
        "own_weights",
        [pack],
        (jax.ShapeDtypeStruct((mols, 2 * width), BF16), weights_of(blocks), f32_rows, f32_rows),
        blocks * tile_flops,
        [one_tile],
    )
    weights = [own_weights] + [None] * len(steps)
    for rank, step in enumerate([1, 0, 2]):
        offsets = steps[step][1]
        last = rank + 1 == len(steps)
        if rank == 0:
            seed_rows, seeds = kernel_call(
                seeds_kernel, "seeds", [seed_mask.reshape(chunks, LANES), profiles, row_sum], (f32_rows, bf16_rows), 1
            )
            peer_seeds = [to_peer(seeds, step) for step in range(min(2, len(steps)))]
        ins = [pack, peer_packs[step], hl, row_sum, col_sum]
        degrees = jax.ShapeDtypeStruct((2 * chunks, LANES), F32)
        out = kernel_call(
            lambda *refs, offsets=offsets, last=last: peer_weights_kernel((blocks, last), offsets, *refs),
            "peer_weights",
            ins,
            (weights_of(blocks * blocks), degrees) if last else (weights_of(blocks * blocks), f32_rows, f32_rows),
            blocks * blocks * tile_flops,
            [pltpu.VMEM((mols, LANES), F32)] * 2 + [one_tile] if last else [one_tile],
        )
        weights[1 + step] = out[0]
        if last:
            degree = out[1]
        else:
            row_sum, col_sum = out[1:]
        if rank == 0:
            held_seeds, row_sum = lax.optimization_barrier((peer_seeds[0], row_sum))
            peer_seeds.append(lax.ppermute(held_seeds, ("row", "col"), list(steps[2][0].items())))
    scales = kernel_call(degree_kernel, "degree", [degree, other_core(degree)], degrees, 1)
    peer_scales = [to_peer(scales, step) for step in range(len(steps) - 1)]
    held_scales, peer_seeds[0] = lax.optimization_barrier((scales, peer_seeds[0]))
    peer_scales.append(to_peer(held_scales, len(steps) - 1))
    own_scales, peer_seeds[1] = lax.optimization_barrier((scales, peer_seeds[1]))
    scaled, row_scale, col_scale = kernel_call(
        expand_kernel, "expand", [own_scales, seed_rows], (bf16_rows, f32_rows, f32_rows), 1
    )
    for iteration in range(ITERS):
        first = iteration == 0
        peers = peer_seeds if first else from_peers(scaled, FORWARD[2])
        partial = kernel_call(
            lambda *refs: product_kernel(blocks, None, False, *refs),
            "own_product",
            [pack, weights[0], scaled],
            f32_rows,
            blocks * tile_flops,
        )
        if not first:
            held, partial = lax.optimization_barrier((scaled, partial))
            peers[1] = to_peer(held, 1)
        for step in [1, 0, 2]:
            offsets = steps[step][1]
            final = step + 1 == len(steps)
            partial = kernel_call(
                lambda *refs, offsets=offsets, first=first: product_kernel(blocks, offsets, first, *refs),
                "peer_product",
                [pack, weights[1 + step], peers[step]] + [peer_scales[step]] * first + [partial],
                bf16_rows if final else f32_rows,
                blocks * blocks * tile_flops,
                [pltpu.VMEM((mols, LANES), BF16)] * first,
            )
        other = other_core(partial)
        if iteration + 1 < ITERS:
            scaled = kernel_call(
                state_kernel, "state", [partial, other, row_scale, seed_rows, col_scale], bf16_rows, 1
            )
    return (partial.astype(F32) + other.astype(F32)) * row_scale + (1.0 - ALPHA) * seed_rows


def solution(mesh):
    placed = (
        P(("grp", "row"), None),
        P(("grp", "row"), None),
        P(("grp", "row")),
        P(("grp", "row"), None),
        P(("grp", "row")),
    )
    return jax.shard_map(
        shards, mesh=mesh, in_specs=placed, out_specs=P(("grp", "row"), None), check_vma=False
    )
```
